128 devices in a mesh: gx: 8 (over z, core), gy: 16 (over x, y).
Axes of the slice: x: 4, y: 4, z: 4, core: 2. Of those that a mesh axis runs over, the one named last changes fastest.
Arguments:
- start_block: float32 [8, 16, 64, 16, 128], P('gx', 'gy')
- tiles: float32 [8, 16, 64, 4, 128, 128], P('gx', 'gy'), may hold values from -0.15625 to 0.15625
- tile_cols: int32 [8, 16, 64, 4], P('gx', 'gy'), may hold values from 0 to 63
- node_diag: float32 [8, 16, 64, 128], P('gx', 'gy'), may hold values from 3 to 24
- face_tiles: float32 [8, 16, 2, 24, 128, 128], P('gx', 'gy'), may hold values from -0.15625 to 0.15625
- face_rows: int32 [8, 16, 4, 24], P('gx', 'gy'), may hold values from 0 to 63, as said below
- filter_bounds: float32 [2], replicated, may hold values from 8 to 30, as said below
Outputs:
- basis: float32 [8, 16, 64, 16, 128], P('gx', 'gy')
- projected: float32 [16, 16], replicated
The draws below stay inside these ranges and needn't reach their ends.
Inputs may be any that keep to these rules, and one draw needn't show every extreme that they name: `tile_cols`: each stored tile's column is a tile row of the same subdomain. `face_rows`: each of the four lists of a subdomain names 24 distinct tile rows. `filter_bounds`: entry 0 lies in 8 to 10 and entry 1 in 26 to 30.
All inputs are finite; a program needn't handle non-finite values.
Results may differ from the reference program's by a relative error of at most 0.0003.
Values sent between devices are 32-bit elements; how exact they have to be, the bound alone decides.
A program may use at most 128 MiB of HBM per device.

```python
import math
import jax
import jax.numpy as jnp
from jax import lax

COLS = 16
TILE = 128
NB = 4
TROWS = 64
FROWS = 24
SUB_X = 8
SUB_Y = 16


def draw_start_block(key, part):
    key = jax.random.fold_in(key, 11)
    shape = (SUB_X, SUB_Y, TROWS, COLS, TILE)
    base = jax.random.normal(key, shape, jnp.float32)
    along_x = jnp.arange(SUB_X, dtype=jnp.float32)[:, None] / max(SUB_X - 1, 1)
    along_y = jnp.arange(SUB_Y, dtype=jnp.float32)[None, :] / max(SUB_Y - 1, 1)
    scale = 1.0 + along_x + along_y
    return base * scale[:, :, None, None, None]


def draw_face_rows(key, part):
    key = jax.random.fold_in(key, 23)
    scores = jax.random.randint(key, (SUB_X, SUB_Y, 4, TROWS), 0, 1 << 16, dtype=jnp.int32)
    scores = scores * TROWS + jnp.arange(TROWS, dtype=jnp.int32)
    order = jnp.argsort(scores, axis=-1, stable=True)
    return order[..., :FROWS].astype(jnp.int32)


def draw_filter_bounds(key, part):
    key = jax.random.fold_in(key, 37)
    shares = jax.random.uniform(key, (2,), jnp.float32)
    return jnp.array([8.0, 26.0], jnp.float32) + shares * jnp.array([2.0, 4.0], jnp.float32)


def plant(values, stream_key, smallest, largest):
    longest = values.shape.index(max(values.shape))
    spots = []
    for shift in (0, 1):
        where = [jax.random.randint(jax.random.fold_in(stream_key, axis), (), 0, length) for axis, length in enumerate(values.shape)]
        where[longest] = (where[longest] + shift) % values.shape[longest]
        spots.append(tuple(where))
    return values.at[spots[0]].set(smallest).at[spots[1]].set(largest)


def block_levels(key, extent, shards, smallest, top_value):
    factor_of, own = 1.0, jax.random.fold_in(key, 6)
    for dim, blocks in shards:
        draws = jnp.exp(jax.random.uniform(jax.random.fold_in(own, dim), (blocks,), jnp.float32, smallest / len(shards), top_value / len(shards)))
        factor_of = factor_of * jnp.repeat(draws, extent[dim] // blocks).reshape([-1 if axis == dim else 1 for axis in range(len(extent))])
    return factor_of


def noise(own_key, extent, scale, reach, pieces=(), kind=jnp.bfloat16):
    drawn = scale * jax.random.normal(own_key, extent, jnp.float32)
    if pieces:
        drawn = drawn * block_levels(own_key, extent, pieces, -0.22, 0.18)
    return jnp.clip(drawn, -reach, reach).astype(kind)


def setup_inputs(seed: int = 0) -> dict:
    arg_keys = jax.random.split(jax.random.key(seed), 8)
    return {
        "start_block": draw_start_block(jax.random.fold_in(arg_keys[7], 71), 0),
        "tiles": noise(arg_keys[1], (SUB_X, SUB_Y, TROWS, NB, TILE, TILE), (2 * NB * TILE + 2 * TILE) ** -0.5, 0.15625, ((0, 8), (1, 16)), jnp.float32),
        "tile_cols": plant(jax.random.randint(arg_keys[2], (SUB_X, SUB_Y, TROWS, NB), 0, TROWS), jax.random.fold_in(arg_keys[2], 1), 0, TROWS - 1).astype(jnp.int32),
        "node_diag": jnp.clip(jnp.exp(math.log(24.0) - 2.0794415 * jax.random.uniform(arg_keys[3], (SUB_X, SUB_Y, TROWS, TILE), jnp.float32) ** block_levels(arg_keys[3], (SUB_X, SUB_Y, TROWS, TILE), ((0, 8), (1, 16)), -0.2, 0.2)), 3.0, 24.0),
        "face_tiles": noise(arg_keys[4], (SUB_X, SUB_Y, 2, FROWS, TILE, TILE), (2 * NB * TILE + 2 * TILE) ** -0.5, 0.15625, ((0, 8), (1, 16)), jnp.float32),
        "face_rows": draw_face_rows(jax.random.fold_in(arg_keys[7], 71), 0),
        "filter_bounds": draw_filter_bounds(jax.random.fold_in(arg_keys[7], 71), 0),
    }


HIGH = lax.Precision.HIGHEST

def local_apply(block, tiles, cols, diag):
    count = block.shape[0]
    gathered = block[cols]
    forward = jnp.einsum('rkcb,rkab->rca', gathered, tiles, precision=HIGH)
    terms = jnp.einsum('rca,rkab->rkcb', block, tiles, precision=HIGH)
    onehot = (cols.reshape(-1)[:, None] == jnp.arange(count, dtype=jnp.int32)[None, :]).astype(block.dtype)
    backward = jnp.einsum('mr,mcb->rcb', onehot, terms.reshape((-1,) + terms.shape[2:]), precision=HIGH)
    return diag[:, None, :] * block + forward + backward

def place(rows, data, count):
    onehot = (rows[:, None] == jnp.arange(count, dtype=jnp.int32)[None, :]).astype(data.dtype)
    return jnp.einsum('fr,fcn->rcn', onehot, data, precision=HIGH)

def face_terms(block, face_tiles, face_rows, axis):
    if axis == 0:
        plus_face, minus_face, which = (0, 1, 0)
    else:
        plus_face, minus_face, which = (2, 3, 1)
    count = block.shape[2]
    length = block.shape[axis]
    pick = jax.vmap(jax.vmap(lambda one, rows: one[rows]))
    minus = pick(block, face_rows[:, :, minus_face])
    plus = pick(block, face_rows[:, :, plus_face])
    coupling = face_tiles[:, :, which]
    upper = jnp.concatenate([lax.slice_in_dim(minus, 1, length, axis=axis), jnp.zeros_like(lax.slice_in_dim(minus, 0, 1, axis=axis))], axis=axis)
    gain = jnp.einsum('uvfcb,uvfab->uvfca', upper, coupling, precision=HIGH)
    outgoing = jnp.einsum('uvfca,uvfab->uvfcb', plus, coupling, precision=HIGH)
    lower = jnp.concatenate([jnp.zeros_like(lax.slice_in_dim(outgoing, 0, 1, axis=axis)), lax.slice_in_dim(outgoing, 0, length - 1, axis=axis)], axis=axis)
    placer = jax.vmap(jax.vmap(lambda rows, data: place(rows, data, count)))
    return placer(face_rows[:, :, plus_face], gain) + placer(face_rows[:, :, minus_face], lower)

def reference(start_block, tiles, tile_cols, node_diag, face_tiles, face_rows, filter_bounds):

    def operate(block):
        total = jax.vmap(jax.vmap(local_apply))(block, tiles, tile_cols, node_diag)
        total = total + face_terms(block, face_tiles, face_rows, 0)
        return total + face_terms(block, face_tiles, face_rows, 1)
    half = (filter_bounds[1] - filter_bounds[0]) / 2.0
    centre = (filter_bounds[1] + filter_bounds[0]) / 2.0
    first = (operate(start_block) - centre * start_block) / half
    second = 2.0 * (operate(first) - centre * first) / half - start_block
    filtered = 2.0 * (operate(second) - centre * second) / half - first
    nodes = filtered.shape[0] * filtered.shape[1] * filtered.shape[2] * filtered.shape[4]
    gram = jnp.einsum('uvrcn,uvrdn->cd', filtered, filtered, precision=HIGH) / nodes
    factor = jnp.linalg.cholesky(gram)
    identity = jnp.eye(gram.shape[0], dtype=gram.dtype)
    inverse = lax.linalg.triangular_solve(factor, identity, left_side=True, lower=True)
    basis = jnp.einsum('cd,uvrdn->uvrcn', inverse, filtered, precision=HIGH)
    image = operate(basis)
    raw = jnp.einsum('uvrcn,uvrdn->cd', basis, image, precision=HIGH) / nodes
    projected = (raw + raw.T) / 2.0
    return (basis, projected)
```

```python
import functools

import jax
import jax.numpy as jnp
from jax import lax
from jax.experimental import pallas as pl
from jax.experimental.pallas import tpu as pltpu
from jax.sharding import PartitionSpec as P

MESH = pl.DeviceIdType.MESH
f32, bf16 = jnp.float32, jnp.bfloat16
NN = (((1,), (0,)), ((), ()))
NT = (((1,), (1,)), ((), ()))
ROWS, NB, COLS, TILE, FROWS = 64, 4, 16, 128, 24
GROUP = 8
NGROUPS = ROWS // GROUP
LOCAL = ROWS * NB
TERMS = 336


def dot(a, b, dims=NN):
    return lax.dot_general(a, b, dims, preferred_element_type=f32)


def split(x):
    high = x.astype(bf16)
    return high, (x - high.astype(f32)).astype(bf16)


def stacked(x):
    return jnp.concatenate(split(x), axis=0)


def times(pair, high, low, dims=NN):
    both = dot(pair, high, dims)
    return both[:COLS] + both[COLS:] + dot(pair[:COLS], low, dims)


def exact(a, b, dims):
    return lax.dot_general(
        a, b, dims, precision=lax.Precision.HIGHEST, preferred_element_type=f32
    )


def kernel(
    gx, gy,
    cols_s, rows_s, bounds_s, cols_v, rows_v, diag, start_h, tiles_h, faces_h,
    basis_h, proj,
    stage, fstage, tn_h, tn_l, tt_h, tt_l, cn_h, cn_l, ct_h, ct_l,
    vb, vs, acc, scat, terms, low, down_s, down_r, up_s, hot, ys, fys,
    pad, gbuf1, gbuf2, sbuf1, sbuf2,
    stage_sem, fstage_sem, start_sem, out_sem,
    down_ss, down_rs, up_ss, up_rs, red_ss, red_rs,
):
    u, v = lax.axis_index("gx"), lax.axis_index("gy")
    nodes = float(gx * gy * ROWS * TILE)

    def stage_copy(group):
        slot = lax.rem(group, 2)
        return pltpu.make_async_copy(
            tiles_h.at[pl.ds(group * GROUP, GROUP)], stage.at[slot], stage_sem.at[slot]
        )

    start_copy = pltpu.make_async_copy(start_h, vb.at[0], start_sem)
    start_copy.start()
    face_copy = pltpu.make_async_copy(faces_h, fstage, fstage_sem)
    face_copy.start()
    stage_copy(0).start()
    stage_copy(1).start()

    barrier = pltpu.get_barrier_semaphore()
    for step in range(1, gx):
        pl.semaphore_signal(
            barrier, inc=1, device_id=(lax.rem(u + step, gx), v), device_id_type=MESH
        )
    for step in range(1, gy):
        pl.semaphore_signal(
            barrier, inc=1, device_id=(u, lax.rem(v + step, gy)), device_id_type=MESH
        )

    lower = (lax.rem(u + gx - 1, gx), v), (u, lax.rem(v + gy - 1, gy))
    upper = (lax.rem(u + 1, gx), v), (u, lax.rem(v + 1, gy))

    def down_copy(axis, slot):
        return pltpu.make_async_remote_copy(
            src_ref=down_s.at[slot, axis], dst_ref=down_r.at[slot, axis],
            send_sem=down_ss.at[slot, axis], recv_sem=down_rs.at[slot, axis],
            device_id=lower[axis], device_id_type=MESH,
        )

    def up_copy(axis, slot):
        return pltpu.make_async_remote_copy(
            src_ref=up_s.at[slot, axis], dst_ref=low.at[slot, axis],
            send_sem=up_ss.at[slot, axis], recv_sem=up_rs.at[slot, axis],
            device_id=upper[axis], device_id_type=MESH,
        )

    wide = lax.broadcasted_iota(jnp.int32, (ROWS, ROWS), 1)
    tall = lax.broadcasted_iota(jnp.int32, (ROWS, FROWS), 0)
    for k in range(NB):
        match = (cols_v[:, k : k + 1] == wide).astype(f32)
        hot[:, k * ROWS : (k + 1) * ROWS] = jnp.transpose(match)
    hot[:, LOCAL:] = jnp.zeros((ROWS, 128), f32)
    has_upper = ((u < gx - 1).astype(f32), (v < gy - 1).astype(f32))
    has_lower = ((u > 0).astype(f32), (v > 0).astype(f32))
    for axis in range(2):
        gain = (rows_v[2 * axis : 2 * axis + 1, :] == tall).astype(f32) * has_upper[axis]
        hot[:, LOCAL + axis * FROWS : LOCAL + (axis + 1) * FROWS] = gain
        lost = (rows_v[2 * axis + 1 : 2 * axis + 2, :] == tall).astype(f32) * has_lower[axis]
        hot[:, TERMS + axis * FROWS : TERMS + (axis + 1) * FROWS] = lost
    terms[(LOCAL + 2 * FROWS) * COLS :, :] = jnp.zeros(
        ((TERMS - LOCAL - 2 * FROWS) * COLS, TILE), f32
    )
    pad[...] = jnp.zeros((COLS, 128), f32)

    low_end = jnp.full((COLS, TILE), bounds_s[0], f32)
    high_end = jnp.full((COLS, TILE), bounds_s[1], f32)
    inverse_half = 2.0 / (high_end - low_end)
    centre = (high_end + low_end) * 0.5

    start_copy.wait()

    def split_rows(i, _):
        vs[i] = stacked(vb[0, i])
        return 0

    lax.fori_loop(0, ROWS, split_rows, 0, unroll=8)

    def fill_down(k, slot):
        def one(j, _):
            for axis in range(2):
                down_s[slot, axis, j] = vb[k, rows_s[2 * axis + 1, j]]
            return 0

        lax.fori_loop(0, FROWS, one, 0, unroll=8)

    def products(slot, axis, first):
        def one(j, _):
            f = axis * FROWS + j
            if first:
                high, small = split(fstage[f])
                cn_h[f] = high
                cn_l[f] = small
                ct_h[f] = jnp.transpose(high)
                ct_l[f] = jnp.transpose(small)
            else:
                high, small = cn_h[f], cn_l[f]
            up_s[slot, axis, j] = times(vs[rows_s[2 * axis, j]], high, small)
            return 0

        lax.fori_loop(0, FROWS, one, 0, unroll=8)

    def gather4(i):
        return jnp.concatenate([vs[cols_s[i, k]] for k in range(NB)], axis=1)

    def convert_row(i, slot, r):
        for k in range(NB):
            high, small = split(stage[slot, r, k])
            lanes = slice(k * TILE, (k + 1) * TILE)
            tn_h[i, :, lanes] = high
            tn_l[i, :, lanes] = small
            tt_h[i, lanes, :] = jnp.transpose(high)
            tt_l[i, lanes, :] = jnp.transpose(small)

    def full_row(i):
        acc[i] = times(gather4(i), tt_h[i], tt_l[i])
        back = times(vs[i], tn_h[i], tn_l[i])
        for k in range(NB):
            at = pl.multiple_of((k * ROWS + i) * COLS, COLS)
            terms[pl.ds(at, COLS), :] = back[:, k * TILE : (k + 1) * TILE]

    def gains(slot):
        def one(j, _):
            for axis in range(2):
                f = axis * FROWS + j
                at = pl.multiple_of((LOCAL + f) * COLS, COLS)
                terms[pl.ds(at, COLS), :] = times(
                    stacked(down_r[slot, axis, j]), ct_h[f], ct_l[f]
                )
            return 0

        lax.fori_loop(0, FROWS, one, 0, unroll=8)

    def scatter(slot):
        places = hot[...].astype(bf16)
        got = low.at[slot].reshape(2 * FROWS * COLS, TILE)
        for c in range(COLS):
            column = jnp.concatenate(
                [
                    terms[pl.ds(c, TERMS, stride=COLS), :],
                    got[pl.ds(c, 2 * FROWS, stride=COLS), :],
                ],
                axis=0,
            )
            out = dot(places, jnp.concatenate(split(column), axis=1))
            scat[pl.ds(c, ROWS, stride=COLS), :] = out[:, :TILE] + out[:, TILE:]

    def update(k, before, scale, keep):
        def one(i, _):
            block = vb[k, i]
            at = pl.multiple_of(i * COLS, COLS)
            applied = diag[pl.ds(i, 1), :] * block + acc[i] + scat[pl.ds(at, COLS), :]
            new = scale * (applied - centre * block)
            if keep:
                new = new - vb[before, i]
            vb[k + 1, i] = new
            vs[i] = stacked(new)
            return 0

        lax.fori_loop(0, ROWS, one, 0, unroll=8)

    def apply(k, first):
        slot = lax.rem(k, 2)
        fill_down(k, slot)
        if first:
            pl.semaphore_wait(barrier, gx + gy - 2)
            face_copy.wait()
        down_copy(1, slot).start()
        down_copy(0, slot).start()
        for axis in (1, 0):
            products(slot, axis, first)
            up_copy(axis, slot).start()

        def group(g, _):
            if first:
                stage_copy(g).wait()
                half_slot = lax.rem(g, 2)

                def row(r, _):
                    i = g * GROUP + r
                    convert_row(i, half_slot, r)
                    full_row(i)
                    return 0

                lax.fori_loop(0, GROUP, row, 0, unroll=True)

                @pl.when(g < NGROUPS - 2)
                def _():
                    stage_copy(g + 2).start()
            else:

                def row(r, _):
                    full_row(g * GROUP + r)
                    return 0

                lax.fori_loop(0, GROUP, row, 0, unroll=True)
            return 0

        lax.fori_loop(0, NGROUPS, group, 0)
        for axis in range(2):
            down_copy(axis, slot).wait()
        gains(slot)
        for axis in range(2):
            up_copy(axis, slot).wait()
        scatter(slot)

    apply(0, True)
    update(0, 0, inverse_half, False)

    def later(k, _):
        apply(k, False)
        update(k, k - 1, 2.0 * inverse_half, True)
        return 0

    lax.fori_loop(1, 3, later, 0)

    def pack(x):
        pad[:, 0:COLS] = x
        full = pad[...]
        return full[:8] + pltpu.roll(full[8:], 64, 1)

    lanes = lax.broadcasted_iota(jnp.int32, (8, 128), 1)

    def unpack(p):
        top = jnp.where(lanes < COLS, p, 0.0)
        bottom = jnp.where(lanes < COLS, pltpu.roll(p, 64, 1), 0.0)
        return jnp.concatenate([top, bottom], axis=0)

    def reduce_copy(which, stage_no, step):
        buffer = ((gbuf1, gbuf2), (sbuf1, sbuf2))[which][stage_no]
        base = which * (gx + gy) + stage_no * gx
        peer = (lax.rem(u + step, gx), v) if stage_no == 0 else (u, lax.rem(v + step, gy))
        return pltpu.make_async_remote_copy(
            src_ref=buffer.at[0], dst_ref=buffer.at[step],
            send_sem=red_ss.at[base + step], recv_sem=red_rs.at[base + step],
            device_id=peer, device_id_type=MESH,
        )

    def reduce_start(which, stage_no, value):
        buffer = ((gbuf1, gbuf2), (sbuf1, sbuf2))[which][stage_no]
        buffer[0] = value
        for step in range(1, (gx, gy)[stage_no]):
            reduce_copy(which, stage_no, step).start()

    def reduce_end(which, stage_no):
        size, me = ((gx, u), (gy, v))[stage_no]
        buffer = ((gbuf1, gbuf2), (sbuf1, sbuf2))[which][stage_no]
        for step in range(1, size):
            reduce_copy(which, stage_no, step).wait()
        total = buffer[me]
        for source in range(1, size):
            total = total + buffer[lax.rem(me + size - source, size)]
        return total

    def inner(count, left, right):
        total = jnp.zeros((COLS, COLS), f32)
        for g in range(count // GROUP):
            a = jnp.concatenate([left(g * GROUP + r) for r in range(GROUP)], axis=1)
            b = jnp.concatenate([right(g * GROUP + r) for r in range(GROUP)], axis=1)
            total = total + times(a, b[:COLS], b[COLS:], NT)
        return total

    fill_down(3, 1)
    down_copy(1, 1).start()
    down_copy(0, 1).start()
    gram = inner(ROWS, lambda i: vs[i], lambda i: vs[i])
    reduce_start(0, 0, pack(gram))

    def half_group(g, _):
        def row(r, _):
            i = g * GROUP + r
            image = times(gather4(i), tt_h[i], tt_l[i])
            image = image + 0.5 * (diag[pl.ds(i, 1), :] * vb[3, i])
            ys[i] = stacked(image)
            return 0

        lax.fori_loop(0, GROUP, row, 0, unroll=True)
        return 0

    lax.fori_loop(0, NGROUPS // 2, half_group, 0)
    reduce_start(0, 1, reduce_end(0, 0))
    lax.fori_loop(NGROUPS // 2, NGROUPS, half_group, 0)
    for axis in range(2):
        down_copy(axis, 1).wait()

    def half_face(j, _):
        for axis in range(2):
            f = axis * FROWS + j
            image = times(stacked(down_r[1, axis, j]), ct_h[f], ct_l[f])
            fys[f] = stacked(image * has_upper[axis])
        return 0

    lax.fori_loop(0, FROWS, half_face, 0, unroll=8)
    half = inner(ROWS, lambda i: vs[i], lambda i: ys[i])
    half = half + inner(
        2 * FROWS, lambda f: vs[rows_s[2 * (f // FROWS), f % FROWS]], lambda f: fys[f]
    )
    reduce_start(1, 0, pack(half))

    work = unpack(reduce_end(0, 1)) * (1.0 / nodes)
    at = lax.broadcasted_iota(jnp.int32, (COLS, 128), 1)
    down = lax.broadcasted_iota(jnp.int32, (COLS, 128), 0)
    work = work + (at == down + 64).astype(f32)
    for j in range(COLS):
        pivot = work[j : j + 1, :]
        root = 1.0 / jnp.sqrt(pivot[:, j : j + 1])
        pivot = pivot * root
        factor = work[:, j : j + 1] * root
        work = jnp.where(down > j, work - factor * pivot, jnp.where(down == j, pivot, work))
    inverse = jnp.where(at < COLS, pltpu.roll(work, 64, 1), 0.0)
    high, small = split(inverse)
    twice = high.astype(f32)
    twice = twice + pltpu.roll(twice, COLS, 1)
    mixer = jnp.concatenate([twice.astype(bf16), small], axis=0)[:, : 2 * COLS]

    reduce_start(1, 1, reduce_end(1, 0))

    for g in range(ROWS // 4):
        four = jnp.concatenate([vs[g * 4 + r] for r in range(4)], axis=1)
        out = dot(mixer, four)
        out = out[:COLS] + out[COLS:]
        for r in range(4):
            vb[0, g * 4 + r] = out[:, r * TILE : (r + 1) * TILE]
    out_copy = pltpu.make_async_copy(vb.at[0], basis_h, out_sem)
    out_copy.start()

    summed = unpack(reduce_end(1, 1))[:, :COLS] * (1.0 / nodes)
    narrow = inverse[:, :COLS]
    both = exact(narrow, summed, NN) + exact(narrow, summed, NT)
    proj[...] = exact(both, narrow, NT)
    out_copy.wait()


def run(gx, gy, cols, rows, bounds, diag, start, tiles, faces):
    hbm = pl.BlockSpec(memory_space=pl.ANY)
    vmem = pl.BlockSpec(memory_space=pltpu.VMEM)
    smem = pl.BlockSpec(memory_space=pltpu.SMEM)
    faces_n = 2 * FROWS
    return pl.pallas_call(
        functools.partial(kernel, gx, gy),
        out_shape=(
            jax.ShapeDtypeStruct((ROWS, COLS, TILE), f32),
            jax.ShapeDtypeStruct((COLS, COLS), f32),
        ),
        in_specs=[smem, smem, smem, vmem, vmem, vmem, hbm, hbm, hbm],
        out_specs=(hbm, vmem),
        scratch_shapes=[
            pltpu.VMEM((2, GROUP, NB, TILE, TILE), f32),
            pltpu.VMEM((faces_n, TILE, TILE), f32),
            pltpu.VMEM((ROWS, TILE, NB * TILE), bf16),
            pltpu.VMEM((ROWS, TILE, NB * TILE), bf16),
            pltpu.VMEM((ROWS, NB * TILE, TILE), bf16),
            pltpu.VMEM((ROWS, NB * TILE, TILE), bf16),
            pltpu.VMEM((faces_n, TILE, TILE), bf16),
            pltpu.VMEM((faces_n, TILE, TILE), bf16),
            pltpu.VMEM((faces_n, TILE, TILE), bf16),
            pltpu.VMEM((faces_n, TILE, TILE), bf16),
            pltpu.VMEM((4, ROWS, COLS, TILE), f32),
            pltpu.VMEM((ROWS, 2 * COLS, TILE), bf16),
            pltpu.VMEM((ROWS, COLS, TILE), f32),
            pltpu.VMEM((ROWS * COLS, TILE), f32),
            pltpu.VMEM((TERMS * COLS, TILE), f32),
            pltpu.VMEM((2, 2, FROWS, COLS, TILE), f32),
            pltpu.VMEM((2, 2, FROWS, COLS, TILE), f32),
            pltpu.VMEM((2, 2, FROWS, COLS, TILE), f32),
            pltpu.VMEM((2, 2, FROWS, COLS, TILE), f32),
            pltpu.VMEM((ROWS, 384), f32),
            pltpu.VMEM((ROWS, 2 * COLS, TILE), bf16),
            pltpu.VMEM((faces_n, 2 * COLS, TILE), bf16),
            pltpu.VMEM((COLS, 128), f32),
            pltpu.VMEM((gx, 8, 128), f32),
            pltpu.VMEM((gy, 8, 128), f32),
            pltpu.VMEM((gx, 8, 128), f32),
            pltpu.VMEM((gy, 8, 128), f32),
            pltpu.SemaphoreType.DMA((2,)),
            pltpu.SemaphoreType.DMA,
            pltpu.SemaphoreType.DMA,
            pltpu.SemaphoreType.DMA,
            pltpu.SemaphoreType.DMA((2, 2)),
            pltpu.SemaphoreType.DMA((2, 2)),
            pltpu.SemaphoreType.DMA((2, 2)),
            pltpu.SemaphoreType.DMA((2, 2)),
            pltpu.SemaphoreType.DMA((2 * (gx + gy),)),
            pltpu.SemaphoreType.DMA((2 * (gx + gy),)),
        ],
        compiler_params=pltpu.CompilerParams(
            collective_id=0, has_side_effects=True, vmem_limit_bytes=62 << 20
        ),
    )(cols, rows, bounds, cols, rows, diag, start, tiles, faces)


def shards(start_block, tiles, tile_cols, node_diag, face_tiles, face_rows, filter_bounds):
    gx, gy = lax.axis_size("gx"), lax.axis_size("gy")
    basis, projected = run(
        gx, gy,
        tile_cols[0, 0], face_rows[0, 0], filter_bounds, node_diag[0, 0], start_block[0, 0],
        tiles[0, 0], face_tiles[0, 0].reshape(2 * FROWS, TILE, TILE),
    )
    return basis[None, None], projected


def solution(mesh):
    in_specs = (
        P("gx", "gy", None, None, None),
        P("gx", "gy", None, None, None, None),
        P("gx", "gy", None, None),
        P("gx", "gy", None, None),
        P("gx", "gy", None, None, None, None),
        P("gx", "gy", None, None),
        P(),
    )
    out_specs = (P("gx", "gy", None, None, None), P())
    return jax.shard_map(shards, mesh=mesh, in_specs=in_specs, out_specs=out_specs, check_vma=False)
```

```python
import functools

import jax
import jax.numpy as jnp
from jax import lax
from jax.experimental import pallas as pl
from jax.experimental.pallas import tpu as pltpu
from jax.sharding import PartitionSpec as P

MESH = pl.DeviceIdType.MESH
f32, bf16 = jnp.float32, jnp.bfloat16
NN = (((1,), (0,)), ((), ()))
NT = (((1,), (1,)), ((), ()))
ROWS, NB, COLS, TILE, FROWS = 64, 4, 16, 128, 24
GROUP = 8
NGROUPS = ROWS // GROUP
LOCAL = ROWS * NB
SLOTS = 3
BIG = 16
TERMS = 336


def dot(a, b, dims=NN):
    return lax.dot_general(a, b, dims, preferred_element_type=f32)


def split(x):
    high = x.astype(bf16)
    return high, (x - high.astype(f32)).astype(bf16)


def stacked(x):
    return jnp.concatenate(split(x), axis=0)


def times(pair, high, low, dims=NN):
    both = dot(pair, high, dims)
    return both[:COLS] + both[COLS:] + dot(pair[:COLS], low, dims)


def exact(a, b, dims):
    return lax.dot_general(
        a, b, dims, precision=lax.Precision.HIGHEST, preferred_element_type=f32
    )


def kernel(
    gx, gy,
    cols_h, rows_h, bounds_h, diag_h, start_h, tiles_h, faces_h,
    basis_h, proj,
    cols_s, rows_s, bounds_s, cols_v, rows_v, diag, stage, fstage, tn_h, tn_l, tt_h, tt_l, cn_h, cn_l, ct_h, ct_l,
    vb, vs, acc, scat, terms, low, down_s, down_r, up_s, hot, ys, fys,
    pad, gbuf1, gbuf2, sbuf1, sbuf2,
    stage_sem, fstage_sem, start_sem, small_sem, out_sem,
    down_ss, down_rs, up_ss, up_rs, red_ss, red_rs,
):
    u, v = lax.axis_index("gx"), lax.axis_index("gy")
    nodes = float(gx * gy * ROWS * TILE)

    def stage_copy(group):
        slot = lax.rem(group, SLOTS)
        return pltpu.make_async_copy(
            tiles_h.at[pl.ds(group * GROUP, GROUP)], stage.at[slot], stage_sem.at[slot]
        )

    pairs = (
        (cols_h, cols_v), (rows_h, rows_v), (rows_h, rows_s), (cols_h, cols_s),
        (bounds_h, bounds_s), (diag_h, diag),
    )
    small = [pltpu.make_async_copy(a, b, small_sem.at[n]) for n, (a, b) in enumerate(pairs)]
    for copy in small[:2]:
        copy.start()
    start_copy = pltpu.make_async_copy(start_h, vb.at[0], start_sem)
    start_copy.start()
    for copy in small[2:]:
        copy.start()
    face_copy = pltpu.make_async_copy(faces_h, fstage, fstage_sem)
    face_copy.start()
    stage_copy(0).start()
    stage_copy(1).start()
    stage_copy(2).start()

    barrier = pltpu.get_barrier_semaphore()
    for step in range(1, gx):
        pl.semaphore_signal(
            barrier, inc=1, device_id=(lax.rem(u + step, gx), v), device_id_type=MESH
        )
    for step in range(1, gy):
        pl.semaphore_signal(
            barrier, inc=1, device_id=(u, lax.rem(v + step, gy)), device_id_type=MESH
        )

    lower = (lax.rem(u + gx - 1, gx), v), (u, lax.rem(v + gy - 1, gy))
    upper = (lax.rem(u + 1, gx), v), (u, lax.rem(v + 1, gy))

    def down_copy(axis, slot):
        return pltpu.make_async_remote_copy(
            src_ref=down_s.at[slot, axis], dst_ref=down_r.at[slot, axis],
            send_sem=down_ss.at[slot, axis], recv_sem=down_rs.at[slot, axis],
            device_id=lower[axis], device_id_type=MESH,
        )

    def up_copy(axis, slot):
        return pltpu.make_async_remote_copy(
            src_ref=up_s.at[slot, axis], dst_ref=low.at[slot, axis],
            send_sem=up_ss.at[slot, axis], recv_sem=up_rs.at[slot, axis],
            device_id=upper[axis], device_id_type=MESH,
        )

    tall = lax.broadcasted_iota(jnp.int32, (ROWS, FROWS), 0)
    taller = lax.broadcasted_iota(jnp.int32, (ROWS, ROWS), 0)
    for copy in small:
        copy.wait()
    for k in range(NB):
        match = (cols_v[k : k + 1, :] == taller).astype(f32)
        hot[:, k * ROWS : (k + 1) * ROWS] = match
    hot[:, LOCAL:] = jnp.zeros((ROWS, 128), f32)
    has_upper = ((u < gx - 1).astype(f32), (v < gy - 1).astype(f32))
    has_lower = ((u > 0).astype(f32), (v > 0).astype(f32))
    for axis in range(2):
        gain = (rows_v[2 * axis : 2 * axis + 1, :] == tall).astype(f32) * has_upper[axis]
        hot[:, LOCAL + axis * FROWS : LOCAL + (axis + 1) * FROWS] = gain
        lost = (rows_v[2 * axis + 1 : 2 * axis + 2, :] == tall).astype(f32) * has_lower[axis]
        hot[:, TERMS + axis * FROWS : TERMS + (axis + 1) * FROWS] = lost
    terms[(LOCAL + 2 * FROWS) * COLS :, :] = jnp.zeros(
        ((TERMS - LOCAL - 2 * FROWS) * COLS, TILE), f32
    )
    pad[...] = jnp.zeros((COLS, 128), f32)

    low_end = jnp.full((COLS, TILE), bounds_s[0], f32)
    high_end = jnp.full((COLS, TILE), bounds_s[1], f32)
    inverse_half = 2.0 / (high_end - low_end)
    centre = (high_end + low_end) * 0.5

    start_copy.wait()

    def split_rows(i, _):
        vs[i] = stacked(vb[0, i])
        return 0

    lax.fori_loop(0, ROWS, split_rows, 0, unroll=8)

    def fill_down(k, slot):
        def one(j, _):
            for axis in range(2):
                down_s[slot, axis, j] = vb[k, rows_s[2 * axis + 1, j]]
            return 0

        lax.fori_loop(0, FROWS, one, 0, unroll=8)

    def products(slot, axis, first):
        def one(j, _):
            f = axis * FROWS + j
            if first:
                high, small = split(fstage[f])
                cn_h[f] = high
                cn_l[f] = small
                ct_h[f] = jnp.transpose(high)
                ct_l[f] = jnp.transpose(small)
            else:
                high, small = cn_h[f], cn_l[f]
            up_s[slot, axis, j] = times(vs[rows_s[2 * axis, j]], high, small)
            return 0

        lax.fori_loop(0, FROWS, one, 0, unroll=True)

    def gather4(i):
        return jnp.concatenate([vs[cols_s[k, i]] for k in range(NB)], axis=1)

    def convert_row(i, slot, r):
        for k in range(NB):
            high, small = split(stage[slot, r, k])
            lanes = slice(k * TILE, (k + 1) * TILE)
            tn_h[i, :, lanes] = high
            tn_l[i, :, lanes] = small
            tt_h[i, lanes, :] = jnp.transpose(high)
            tt_l[i, lanes, :] = jnp.transpose(small)

    def full_row(i):
        acc[i] = times(gather4(i), tt_h[i], tt_l[i])
        back = times(vs[i], tn_h[i], tn_l[i])
        for k in range(NB):
            at = pl.multiple_of((k * ROWS + i) * COLS, COLS)
            terms[pl.ds(at, COLS), :] = back[:, k * TILE : (k + 1) * TILE]

    def gains(slot):
        def one(j, _):
            for axis in range(2):
                f = axis * FROWS + j
                at = pl.multiple_of((LOCAL + f) * COLS, COLS)
                terms[pl.ds(at, COLS), :] = times(
                    stacked(down_r[slot, axis, j]), ct_h[f], ct_l[f]
                )
            return 0

        lax.fori_loop(0, FROWS, one, 0, unroll=True)

    def scatter(slot):
        places = hot[...].astype(bf16)
        got = low.at[slot].reshape(2 * FROWS * COLS, TILE)
        for c in range(COLS):
            column = jnp.concatenate(
                [
                    terms[pl.ds(c, TERMS, stride=COLS), :],
                    got[pl.ds(c, 2 * FROWS, stride=COLS), :],
                ],
                axis=0,
            )
            out = dot(places, jnp.concatenate(split(column), axis=1))
            scat[pl.ds(c, ROWS, stride=COLS), :] = out[:, :TILE] + out[:, TILE:]

    def update(k, before, scale, keep):
        def one(i, _):
            block = vb[k, i]
            at = pl.multiple_of(i * COLS, COLS)
            applied = diag[pl.ds(i, 1), :] * block + acc[i] + scat[pl.ds(at, COLS), :]
            new = scale * (applied - centre * block)
            if keep:
                new = new - vb[before, i]
            vb[k + 1, i] = new
            vs[i] = stacked(new)
            return 0

        lax.fori_loop(0, ROWS, one, 0, unroll=8)

    def apply(k, first):
        slot = lax.rem(k, 2)
        fill_down(k, slot)
        if first:
            pl.semaphore_wait(barrier, gx + gy - 2)
            face_copy.wait()
        down_copy(1, slot).start()
        down_copy(0, slot).start()
        for axis in (1, 0):
            products(slot, axis, first)
            up_copy(axis, slot).start()

        def group(g, _):
            stage_copy(g).wait()
            at = lax.rem(g, SLOTS)

            def row(r, _):
                i = g * GROUP + r
                convert_row(i, at, r)
                full_row(i)
                return 0

            lax.fori_loop(0, GROUP, row, 0, unroll=True)

            @pl.when(g < NGROUPS - SLOTS)
            def _():
                stage_copy(g + SLOTS).start()

            return 0

        def plain(i, _):
            full_row(i)
            return 0

        if first:
            lax.fori_loop(0, NGROUPS, group, 0)
        else:
            lax.fori_loop(0, ROWS, plain, 0, unroll=BIG)
        for axis in range(2):
            down_copy(axis, slot).wait()
        gains(slot)
        for axis in range(2):
            up_copy(axis, slot).wait()
        scatter(slot)

    apply(0, True)
    update(0, 0, inverse_half, False)

    def later(k, _):
        apply(k, False)
        update(k, k - 1, 2.0 * inverse_half, True)
        return 0

    lax.fori_loop(1, 3, later, 0)

    def pack(x):
        pad[:, 0 : 2 * COLS] = x[:COLS] + x[COLS:]
        full = pad[...]
        full = jnp.where(at < COLS, full + pltpu.roll(full, 128 - COLS, 1), 0.0)
        return full[:8] + pltpu.roll(full[8:], 64, 1)

    lanes = lax.broadcasted_iota(jnp.int32, (8, 128), 1)
    at = lax.broadcasted_iota(jnp.int32, (COLS, 128), 1)

    def unpack(p):
        top = jnp.where(lanes < COLS, p, 0.0)
        bottom = jnp.where(lanes < COLS, pltpu.roll(p, 64, 1), 0.0)
        return jnp.concatenate([top, bottom], axis=0)

    def reduce_copy(which, stage_no, step):
        buffer = ((gbuf1, gbuf2), (sbuf1, sbuf2))[which][stage_no]
        base = which * (gx + gy) + stage_no * gx
        peer = (lax.rem(u + step, gx), v) if stage_no == 0 else (u, lax.rem(v + step, gy))
        return pltpu.make_async_remote_copy(
            src_ref=buffer.at[0], dst_ref=buffer.at[step],
            send_sem=red_ss.at[base + step], recv_sem=red_rs.at[base + step],
            device_id=peer, device_id_type=MESH,
        )

    def reduce_start(which, stage_no, value):
        buffer = ((gbuf1, gbuf2), (sbuf1, sbuf2))[which][stage_no]
        buffer[0] = value
        for step in range(1, (gx, gy)[stage_no]):
            reduce_copy(which, stage_no, step).start()

    def reduce_end(which, stage_no):
        size, me = ((gx, u), (gy, v))[stage_no]
        buffer = ((gbuf1, gbuf2), (sbuf1, sbuf2))[which][stage_no]
        for step in range(1, size):
            reduce_copy(which, stage_no, step).wait()
        total = buffer[me]
        for source in range(1, size):
            total = total + buffer[lax.rem(me + size - source, size)]
        return total

    def inner(count, left, right):
        total = jnp.zeros((2 * COLS, 2 * COLS), f32)
        for g in range(count // BIG):
            a = jnp.concatenate([left(g * BIG + r) for r in range(BIG)], axis=1)
            b = jnp.concatenate([right(g * BIG + r) for r in range(BIG)], axis=1)
            total = total + dot(a, b, NT)
        return total

    fill_down(3, 1)
    down_copy(1, 1).start()
    down_copy(0, 1).start()
    gram = inner(ROWS, lambda i: vs[i], lambda i: vs[i])
    reduce_start(0, 0, pack(gram))

    def half_row(i, _):
        image = times(gather4(i), tt_h[i], tt_l[i])
        image = image + 0.5 * (diag[pl.ds(i, 1), :] * vb[3, i])
        ys[i] = stacked(image)
        return 0

    lax.fori_loop(0, ROWS // 2, half_row, 0, unroll=BIG)
    reduce_start(0, 1, reduce_end(0, 0))
    lax.fori_loop(ROWS // 2, ROWS, half_row, 0, unroll=BIG)
    for axis in range(2):
        down_copy(axis, 1).wait()

    def half_face(j, _):
        for axis in range(2):
            f = axis * FROWS + j
            image = times(stacked(down_r[1, axis, j]), ct_h[f], ct_l[f])
            fys[f] = stacked(image * has_upper[axis])
        return 0

    lax.fori_loop(0, FROWS, half_face, 0, unroll=True)
    half = inner(ROWS, lambda i: vs[i], lambda i: ys[i])
    half = half + inner(
        2 * FROWS, lambda f: vs[rows_s[2 * (f // FROWS), f % FROWS]], lambda f: fys[f]
    )
    reduce_start(1, 0, pack(half))

    work = unpack(reduce_end(0, 1)) * (1.0 / nodes)
    down = lax.broadcasted_iota(jnp.int32, (COLS, 128), 0)
    work = work + (at == down + 64).astype(f32)
    for j in range(COLS):
        pivot = work[j : j + 1, :]
        root = 1.0 / jnp.sqrt(pivot[:, j : j + 1])
        pivot = pivot * root
        factor = work[:, j : j + 1] * root
        work = jnp.where(down > j, work - factor * pivot, jnp.where(down == j, pivot, work))
    inverse = jnp.where(at < COLS, pltpu.roll(work, 64, 1), 0.0)
    high, small = split(inverse)
    twice = high.astype(f32)
    twice = twice + pltpu.roll(twice, COLS, 1)
    mixer = jnp.concatenate([twice.astype(bf16), small], axis=0)[:, : 2 * COLS]

    reduce_start(1, 1, reduce_end(1, 0))

    for g in range(ROWS // 4):
        four = jnp.concatenate([vs[g * 4 + r] for r in range(4)], axis=1)
        out = dot(mixer, four)
        out = out[:COLS] + out[COLS:]
        for r in range(4):
            vb[0, g * 4 + r] = out[:, r * TILE : (r + 1) * TILE]
    out_copy = pltpu.make_async_copy(vb.at[0], basis_h, out_sem)
    out_copy.start()

    summed = unpack(reduce_end(1, 1))[:, :COLS] * (1.0 / nodes)
    narrow = inverse[:, :COLS]
    both = exact(narrow, summed, NN) + exact(narrow, summed, NT)
    proj[...] = exact(both, narrow, NT)
    out_copy.wait()


def hand_over(basis_in, proj_in, basis, proj, sem):
    copies = [
        pltpu.make_async_copy(basis_in, basis, sem.at[0]),
        pltpu.make_async_copy(proj_in, proj, sem.at[1]),
    ]
    for copy in copies:
        copy.start()
    for copy in copies:
        copy.wait()


def run(gx, gy, cols, rows, bounds, diag, start, tiles, faces):
    hbm = pl.BlockSpec(memory_space=pl.ANY)
    vmem = pl.BlockSpec(memory_space=pltpu.VMEM)
    faces_n = 2 * FROWS
    shapes = (
        jax.ShapeDtypeStruct((ROWS, COLS, TILE), f32),
        jax.ShapeDtypeStruct((COLS, COLS), f32),
    )
    results = pl.pallas_call(
        functools.partial(kernel, gx, gy),
        out_shape=shapes,
        in_specs=[hbm] * 7,
        out_specs=(hbm, vmem),
        scratch_shapes=[
            pltpu.SMEM((NB, ROWS), jnp.int32),
            pltpu.SMEM((4, FROWS), jnp.int32),
            pltpu.SMEM((2,), f32),
            pltpu.VMEM((NB, ROWS), jnp.int32),
            pltpu.VMEM((4, FROWS), jnp.int32),
            pltpu.VMEM((ROWS, TILE), f32),
            pltpu.VMEM((SLOTS, GROUP, NB, TILE, TILE), f32),
            pltpu.VMEM((faces_n, TILE, TILE), f32),
            pltpu.VMEM((ROWS, TILE, NB * TILE), bf16),
            pltpu.VMEM((ROWS, TILE, NB * TILE), bf16),
            pltpu.VMEM((ROWS, NB * TILE, TILE), bf16),
            pltpu.VMEM((ROWS, NB * TILE, TILE), bf16),
            pltpu.VMEM((faces_n, TILE, TILE), bf16),
            pltpu.VMEM((faces_n, TILE, TILE), bf16),
            pltpu.VMEM((faces_n, TILE, TILE), bf16),
            pltpu.VMEM((faces_n, TILE, TILE), bf16),
            pltpu.VMEM((4, ROWS, COLS, TILE), f32),
            pltpu.VMEM((ROWS, 2 * COLS, TILE), bf16),
            pltpu.VMEM((ROWS, COLS, TILE), f32),
            pltpu.VMEM((ROWS * COLS, TILE), f32),
            pltpu.VMEM((TERMS * COLS, TILE), f32),
            pltpu.VMEM((2, 2, FROWS, COLS, TILE), f32),
            pltpu.VMEM((2, 2, FROWS, COLS, TILE), f32),
            pltpu.VMEM((2, 2, FROWS, COLS, TILE), f32),
            pltpu.VMEM((2, 2, FROWS, COLS, TILE), f32),
            pltpu.VMEM((ROWS, 384), f32),
            pltpu.VMEM((ROWS, 2 * COLS, TILE), bf16),
            pltpu.VMEM((faces_n, 2 * COLS, TILE), bf16),
            pltpu.VMEM((COLS, 128), f32),
            pltpu.VMEM((gx, 8, 128), f32),
            pltpu.VMEM((gy, 8, 128), f32),
            pltpu.VMEM((gx, 8, 128), f32),
            pltpu.VMEM((gy, 8, 128), f32),
            pltpu.SemaphoreType.DMA((SLOTS,)),
            pltpu.SemaphoreType.DMA,
            pltpu.SemaphoreType.DMA,
            pltpu.SemaphoreType.DMA((6,)),
            pltpu.SemaphoreType.DMA,
            pltpu.SemaphoreType.DMA((2, 2)),
            pltpu.SemaphoreType.DMA((2, 2)),
            pltpu.SemaphoreType.DMA((2, 2)),
            pltpu.SemaphoreType.DMA((2, 2)),
            pltpu.SemaphoreType.DMA((2 * (gx + gy),)),
            pltpu.SemaphoreType.DMA((2 * (gx + gy),)),
        ],
        compiler_params=pltpu.CompilerParams(
            collective_id=0, has_side_effects=True, vmem_limit_bytes=62 << 20
        ),
    )(cols, rows, bounds, diag, start, tiles, faces)
    return pl.pallas_call(
        hand_over,
        out_shape=shapes,
        in_specs=[hbm] * 2,
        out_specs=(hbm, hbm),
        scratch_shapes=[pltpu.SemaphoreType.DMA((2,))],
    )(*results)


def shards(start_block, tiles, tile_cols, node_diag, face_tiles, face_rows, filter_bounds):
    gx, gy = lax.axis_size("gx"), lax.axis_size("gy")
    basis, projected = run(
        gx, gy,
        tile_cols[0, 0].T, face_rows[0, 0], filter_bounds, node_diag[0, 0], start_block[0, 0],
        tiles[0, 0], face_tiles[0, 0].reshape(2 * FROWS, TILE, TILE),
    )
    return basis[None, None], projected


def solution(mesh):
    in_specs = (
        P("gx", "gy", None, None, None),
        P("gx", "gy", None, None, None, None),
        P("gx", "gy", None, None),
        P("gx", "gy", None, None),
        P("gx", "gy", None, None, None, None),
        P("gx", "gy", None, None),
        P(),
    )
    out_specs = (P("gx", "gy", None, None, None), P())
    return jax.shard_map(shards, mesh=mesh, in_specs=in_specs, out_specs=out_specs, check_vma=False)
```

```python
import functools

import jax
import jax.numpy as jnp
from jax import lax
from jax.experimental import pallas as pl
from jax.experimental.pallas import tpu as pltpu
from jax.sharding import PartitionSpec as P

MESH = pl.DeviceIdType.MESH
f32, bf16 = jnp.float32, jnp.bfloat16
NN = (((1,), (0,)), ((), ()))
NT = (((1,), (1,)), ((), ()))
ROWS, NB, COLS, TILE, FROWS = 64, 4, 16, 128, 24
GROUP = 8
NGROUPS = ROWS // GROUP
LOCAL = ROWS * NB
SLOTS = 4
BIG = 16
TERMS = 336


def dot(a, b, dims=NN):
    return lax.dot_general(a, b, dims, preferred_element_type=f32)


def split(x):
    high = x.astype(bf16)
    return high, (x - high.astype(f32)).astype(bf16)


def stacked(x):
    return jnp.concatenate(split(x), axis=0)


def times(pair, high, low, dims=NN):
    both = dot(pair, high, dims)
    return both[:COLS] + both[COLS:] + dot(pair[:COLS], low, dims)


def times_wide(pair, both):
    out = dot(pair, both)
    out = out[:COLS] + out[COLS:]
    return out[:, :TILE] + out[:, TILE:]


def exact(a, b, dims):
    return lax.dot_general(
        a, b, dims, precision=lax.Precision.HIGHEST, preferred_element_type=f32
    )


def kernel(
    gx, gy,
    cols_h, rows_h, bounds_h, diag_h, start_h, tiles_h, faces_h,
    basis_h, proj,
    cols_s, rows_s, bounds_s, cols_v, rows_v, diag, stage, fstage,
    tn_h0, tn_l0, tt_h0, tt_l0, tn_h1, tn_l1, tt_h1, tt_l1, cn, ct,
    vb, vs, acc, scat, terms, low, down_s, down_r, up_s, hot, ys, fys,
    pad, gbuf1, gbuf2, sbuf1, sbuf2,
    stage_sem, fstage_sem, start_sem, small_sem, out_sem,
    down_ss, down_rs, up_ss, up_rs, red_ss, red_rs,
):
    u, v = lax.axis_index("gx"), lax.axis_index("gy")
    held = (tn_h0, tn_l0, tt_h0, tt_l0), (tn_h1, tn_l1, tt_h1, tt_l1)
    nodes = float(gx * gy * ROWS * TILE)

    def stage_copy(group):
        slot = lax.rem(group, SLOTS)
        return pltpu.make_async_copy(
            tiles_h.at[pl.ds(group * GROUP, GROUP)], stage.at[slot], stage_sem.at[slot]
        )

    pairs = (
        (cols_h, cols_v), (rows_h, rows_v), (rows_h, rows_s), (cols_h, cols_s),
        (bounds_h, bounds_s), (diag_h, diag),
    )
    small = [pltpu.make_async_copy(a, b, small_sem.at[n]) for n, (a, b) in enumerate(pairs)]
    for copy in small[:2]:
        copy.start()
    start_copy = pltpu.make_async_copy(start_h, vb.at[0], start_sem)
    start_copy.start()
    for copy in small[2:]:
        copy.start()
    face_copy = pltpu.make_async_copy(faces_h, fstage, fstage_sem)
    face_copy.start()
    stage_copy(0).start()
    stage_copy(1).start()
    stage_copy(2).start()
    stage_copy(3).start()

    barrier = pltpu.get_barrier_semaphore()
    for step in range(1, gx):
        pl.semaphore_signal(
            barrier, inc=1, device_id=(lax.rem(u + step, gx), v), device_id_type=MESH
        )
    for step in range(1, gy):
        pl.semaphore_signal(
            barrier, inc=1, device_id=(u, lax.rem(v + step, gy)), device_id_type=MESH
        )

    lower = (lax.rem(u + gx - 1, gx), v), (u, lax.rem(v + gy - 1, gy))
    upper = (lax.rem(u + 1, gx), v), (u, lax.rem(v + 1, gy))

    def down_copy(axis, slot):
        return pltpu.make_async_remote_copy(
            src_ref=down_s.at[slot, axis], dst_ref=down_r.at[slot, axis],
            send_sem=down_ss.at[slot, axis], recv_sem=down_rs.at[slot, axis],
            device_id=lower[axis], device_id_type=MESH,
        )

    def up_copy(axis, slot):
        return pltpu.make_async_remote_copy(
            src_ref=up_s.at[slot, axis], dst_ref=low.at[slot, axis],
            send_sem=up_ss.at[slot, axis], recv_sem=up_rs.at[slot, axis],
            device_id=upper[axis], device_id_type=MESH,
        )

    tall = lax.broadcasted_iota(jnp.int32, (ROWS, FROWS), 0)
    taller = lax.broadcasted_iota(jnp.int32, (ROWS, ROWS), 0)
    for copy in small:
        copy.wait()
    for k in range(NB):
        match = (cols_v[k : k + 1, :] == taller).astype(f32)
        hot[:, k * ROWS : (k + 1) * ROWS] = match
    hot[:, LOCAL:] = jnp.zeros((ROWS, 128), f32)
    has_upper = ((u < gx - 1).astype(f32), (v < gy - 1).astype(f32))
    has_lower = ((u > 0).astype(f32), (v > 0).astype(f32))
    for axis in range(2):
        gain = (rows_v[2 * axis : 2 * axis + 1, :] == tall).astype(f32) * has_upper[axis]
        hot[:, LOCAL + axis * FROWS : LOCAL + (axis + 1) * FROWS] = gain
        lost = (rows_v[2 * axis + 1 : 2 * axis + 2, :] == tall).astype(f32) * has_lower[axis]
        hot[:, TERMS + axis * FROWS : TERMS + (axis + 1) * FROWS] = lost
    terms[(LOCAL + 2 * FROWS) * COLS :, :] = jnp.zeros(
        ((TERMS - LOCAL - 2 * FROWS) * COLS, TILE), f32
    )
    pad[...] = jnp.zeros((COLS, 128), f32)

    low_end = jnp.full((COLS, TILE), bounds_s[0], f32)
    high_end = jnp.full((COLS, TILE), bounds_s[1], f32)
    inverse_half = 2.0 / (high_end - low_end)
    centre = (high_end + low_end) * 0.5

    start_copy.wait()

    def split_rows(i, _):
        vs[i] = stacked(vb[0, i])
        return 0

    lax.fori_loop(0, ROWS, split_rows, 0, unroll=8)

    def fill_down(k, slot):
        def one(j, _):
            for axis in range(2):
                down_s[slot, axis, j] = vb[k, rows_s[2 * axis + 1, j]]
            return 0

        lax.fori_loop(0, FROWS, one, 0, unroll=8)

    def products(slot, axis, first):
        def one(j, _):
            f = axis * FROWS + j
            if first:
                high, small = split(fstage[f])
                both = jnp.concatenate([high, small], axis=1)
                cn[f] = both
                ct[f, :, :TILE] = jnp.transpose(high)
                ct[f, :, TILE:] = jnp.transpose(small)
            else:
                both = cn[f]
            up_s[slot, axis, j] = times_wide(vs[rows_s[2 * axis, j]], both)
            return 0

        lax.fori_loop(0, FROWS, one, 0, unroll=True)

    def gather4(i):
        return jnp.concatenate([vs[cols_s[k, i]] for k in range(NB)], axis=1)

    def convert_row(part, t, slot, r):
        tn_h, tn_l, tt_h, tt_l = held[part]
        for k in range(NB):
            high, small = split(stage[slot, r, k])
            lanes = slice(k * TILE, (k + 1) * TILE)
            tn_h[t, :, lanes] = high
            tn_l[t, :, lanes] = small
            tt_h[t, lanes, :] = jnp.transpose(high)
            tt_l[t, lanes, :] = jnp.transpose(small)

    def full_row(part, t, i):
        tn_h, tn_l, tt_h, tt_l = held[part]
        acc[i] = times(gather4(i), tt_h[t], tt_l[t])
        back = times(vs[i], tn_h[t], tn_l[t])
        for k in range(NB):
            at = pl.multiple_of((k * ROWS + i) * COLS, COLS)
            terms[pl.ds(at, COLS), :] = back[:, k * TILE : (k + 1) * TILE]

    def gains(slot):
        def one(j, _):
            for axis in range(2):
                f = axis * FROWS + j
                at = pl.multiple_of((LOCAL + f) * COLS, COLS)
                terms[pl.ds(at, COLS), :] = times_wide(
                    stacked(down_r[slot, axis, j]), ct[f]
                )
            return 0

        lax.fori_loop(0, FROWS, one, 0, unroll=True)

    def scatter(slot):
        places = hot[...].astype(bf16)
        got = low.at[slot].reshape(2 * FROWS * COLS, TILE)
        for c in range(COLS):
            column = jnp.concatenate(
                [
                    terms[pl.ds(c, TERMS, stride=COLS), :],
                    got[pl.ds(c, 2 * FROWS, stride=COLS), :],
                ],
                axis=0,
            )
            out = dot(places, jnp.concatenate(split(column), axis=1))
            scat[pl.ds(c, ROWS, stride=COLS), :] = out[:, :TILE] + out[:, TILE:]

    def update(k, before, scale, keep):
        def one(i, _):
            block = vb[k, i]
            at = pl.multiple_of(i * COLS, COLS)
            applied = diag[pl.ds(i, 1), :] * block + acc[i] + scat[pl.ds(at, COLS), :]
            new = scale * (applied - centre * block)
            if keep:
                new = new - vb[before, i]
            vb[k + 1, i] = new
            vs[i] = stacked(new)
            return 0

        lax.fori_loop(0, ROWS, one, 0, unroll=8)

    def apply(k, first):
        slot = lax.rem(k, 2)
        fill_down(k, slot)
        if first:
            pl.semaphore_wait(barrier, gx + gy - 2)
            face_copy.wait()
        down_copy(1, slot).start()
        down_copy(0, slot).start()
        for axis in (1, 0):
            products(slot, axis, first)
            up_copy(axis, slot).start()

        def convert_group(part, pair, r):
            convert_row(part, pair * GROUP + r, lax.rem(2 * pair + part, SLOTS), r)

        def full_group(part, pair, r):
            full_row(part, pair * GROUP + r, (2 * pair + part) * GROUP + r)

        if first:
            stage_copy(0).wait()
            for r in range(GROUP):
                convert_group(0, 0, r)

            def two_groups(pair, _):
                @pl.when(pair < NGROUPS // 2 - 2)
                def _():
                    stage_copy(2 * pair + 4).start()

                stage_copy(2 * pair + 1).wait()
                for r in range(GROUP):
                    convert_group(1, pair, r)
                    full_group(0, pair, r)

                @pl.when(pair < NGROUPS // 2 - 2)
                def _():
                    stage_copy(2 * pair + 5).start()

                stage_copy(2 * pair + 2).wait()
                for r in range(GROUP):
                    convert_group(0, pair + 1, r)
                    full_group(1, pair, r)
                return 0

            lax.fori_loop(0, NGROUPS // 2 - 1, two_groups, 0)
            last = NGROUPS // 2 - 1
            stage_copy(NGROUPS - 1).wait()
            for r in range(GROUP):
                convert_group(1, last, r)
                full_group(0, last, r)
            for r in range(GROUP):
                full_group(1, last, r)
        else:

            def plain(pair, _):
                for part in range(2):
                    for r in range(GROUP):
                        full_group(part, pair, r)
                return 0

            lax.fori_loop(0, NGROUPS // 2, plain, 0)
        for axis in range(2):
            down_copy(axis, slot).wait()
        gains(slot)
        for axis in range(2):
            up_copy(axis, slot).wait()
        scatter(slot)

    apply(0, True)
    update(0, 0, inverse_half, False)

    def later(k, _):
        apply(k, False)
        update(k, k - 1, 2.0 * inverse_half, True)
        return 0

    lax.fori_loop(1, 3, later, 0)

    def pack(x):
        pad[:, 0 : 2 * COLS] = x[:COLS] + x[COLS:]
        full = pad[...]
        full = jnp.where(at < COLS, full + pltpu.roll(full, 128 - COLS, 1), 0.0)
        return full[:8] + pltpu.roll(full[8:], 64, 1)

    lanes = lax.broadcasted_iota(jnp.int32, (8, 128), 1)
    at = lax.broadcasted_iota(jnp.int32, (COLS, 128), 1)

    def unpack(p):
        top = jnp.where(lanes < COLS, p, 0.0)
        bottom = jnp.where(lanes < COLS, pltpu.roll(p, 64, 1), 0.0)
        return jnp.concatenate([top, bottom], axis=0)

    def reduce_copy(which, stage_no, step):
        buffer = ((gbuf1, gbuf2), (sbuf1, sbuf2))[which][stage_no]
        base = which * (gx + gy) + stage_no * gx
        peer = (lax.rem(u + step, gx), v) if stage_no == 0 else (u, lax.rem(v + step, gy))
        return pltpu.make_async_remote_copy(
            src_ref=buffer.at[0], dst_ref=buffer.at[step],
            send_sem=red_ss.at[base + step], recv_sem=red_rs.at[base + step],
            device_id=peer, device_id_type=MESH,
        )

    def reduce_start(which, stage_no, value):
        buffer = ((gbuf1, gbuf2), (sbuf1, sbuf2))[which][stage_no]
        buffer[0] = value
        for step in range(1, (gx, gy)[stage_no]):
            reduce_copy(which, stage_no, step).start()

    def reduce_end(which, stage_no):
        size, me = ((gx, u), (gy, v))[stage_no]
        buffer = ((gbuf1, gbuf2), (sbuf1, sbuf2))[which][stage_no]
        for step in range(1, size):
            reduce_copy(which, stage_no, step).wait()
        total = buffer[me]
        for source in range(1, size):
            total = total + buffer[lax.rem(me + size - source, size)]
        return total

    def inner(count, left, right):
        total = jnp.zeros((2 * COLS, 2 * COLS), f32)
        for g in range(count // BIG):
            a = jnp.concatenate([left(g * BIG + r) for r in range(BIG)], axis=1)
            b = jnp.concatenate([right(g * BIG + r) for r in range(BIG)], axis=1)
            total = total + dot(a, b, NT)
        return total

    fill_down(3, 1)
    down_copy(1, 1).start()
    down_copy(0, 1).start()
    gram = inner(ROWS, lambda i: vs[i], lambda i: vs[i])
    reduce_start(0, 0, pack(gram))

    def half_groups(pair, _):
        for part in range(2):
            high, small = held[part][2:]
            for r in range(GROUP):
                i = (2 * pair + part) * GROUP + r
                t = pair * GROUP + r
                image = times(gather4(i), high[t], small[t])
                image = image + 0.5 * (diag[pl.ds(i, 1), :] * vb[3, i])
                ys[i] = stacked(image)
        return 0

    lax.fori_loop(0, NGROUPS // 4, half_groups, 0)
    reduce_start(0, 1, reduce_end(0, 0))
    lax.fori_loop(NGROUPS // 4, NGROUPS // 2, half_groups, 0)
    for axis in range(2):
        down_copy(axis, 1).wait()

    def half_face(j, _):
        for axis in range(2):
            f = axis * FROWS + j
            image = times_wide(stacked(down_r[1, axis, j]), ct[f])
            fys[f] = stacked(image * has_upper[axis])
        return 0

    lax.fori_loop(0, FROWS, half_face, 0, unroll=True)
    half = inner(ROWS, lambda i: vs[i], lambda i: ys[i])
    half = half + inner(
        2 * FROWS, lambda f: vs[rows_s[2 * (f // FROWS), f % FROWS]], lambda f: fys[f]
    )
    reduce_start(1, 0, pack(half))

    work = unpack(reduce_end(0, 1)) * (1.0 / nodes)
    down = lax.broadcasted_iota(jnp.int32, (COLS, 128), 0)
    work = work + (at == down + 64).astype(f32)
    for j in range(COLS):
        pivot = work[j : j + 1, :]
        root = 1.0 / jnp.sqrt(pivot[:, j : j + 1])
        pivot = pivot * root
        factor = work[:, j : j + 1] * root
        work = jnp.where(down > j, work - factor * pivot, jnp.where(down == j, pivot, work))
    inverse = jnp.where(at < COLS, pltpu.roll(work, 64, 1), 0.0)
    high, small = split(inverse)
    twice = high.astype(f32)
    twice = twice + pltpu.roll(twice, COLS, 1)
    mixer = jnp.concatenate([twice.astype(bf16), small], axis=0)[:, : 2 * COLS]

    reduce_start(1, 1, reduce_end(1, 0))

    for g in range(ROWS // 4):
        four = jnp.concatenate([vs[g * 4 + r] for r in range(4)], axis=1)
        out = dot(mixer, four)
        out = out[:COLS] + out[COLS:]
        for r in range(4):
            vb[0, g * 4 + r] = out[:, r * TILE : (r + 1) * TILE]
    out_copy = pltpu.make_async_copy(vb.at[0], basis_h, out_sem)
    out_copy.start()

    summed = unpack(reduce_end(1, 1))[:, :COLS] * (1.0 / nodes)
    narrow = inverse[:, :COLS]
    both = exact(narrow, summed, NN) + exact(narrow, summed, NT)
    proj[...] = exact(both, narrow, NT)
    out_copy.wait()


def hand_over(basis_in, proj_in, basis, proj, held, small, sems):
    parts = ROWS // GROUP
    ins = [
        pltpu.make_async_copy(
            basis_in.at[pl.ds(g * GROUP, GROUP)], held.at[pl.ds(g * GROUP, GROUP)], sems.at[0, g]
        )
        for g in range(parts)
    ] + [pltpu.make_async_copy(proj_in, small, sems.at[0, parts])]
    outs = [
        pltpu.make_async_copy(
            held.at[pl.ds(g * GROUP, GROUP)], basis.at[pl.ds(g * GROUP, GROUP)], sems.at[1, g]
        )
        for g in range(parts)
    ] + [pltpu.make_async_copy(small, proj, sems.at[1, parts])]
    for copy in ins:
        copy.start()
    for first, second in zip(ins, outs):
        first.wait()
        second.start()
    for copy in outs:
        copy.wait()


def run(gx, gy, cols, rows, bounds, diag, start, tiles, faces):
    hbm = pl.BlockSpec(memory_space=pl.ANY)
    vmem = pl.BlockSpec(memory_space=pltpu.VMEM)
    faces_n = 2 * FROWS
    shapes = (
        jax.ShapeDtypeStruct((ROWS, COLS, TILE), f32),
        jax.ShapeDtypeStruct((COLS, COLS), f32),
    )
    results = pl.pallas_call(
        functools.partial(kernel, gx, gy),
        out_shape=shapes,
        in_specs=[hbm] * 7,
        out_specs=(hbm, vmem),
        scratch_shapes=[
            pltpu.SMEM((NB, ROWS), jnp.int32),
            pltpu.SMEM((4, FROWS), jnp.int32),
            pltpu.SMEM((2,), f32),
            pltpu.VMEM((NB, ROWS), jnp.int32),
            pltpu.VMEM((4, FROWS), jnp.int32),
            pltpu.VMEM((ROWS, TILE), f32),
            pltpu.VMEM((SLOTS, GROUP, NB, TILE, TILE), f32),
            pltpu.VMEM((faces_n, TILE, TILE), f32),
            *(
                [pltpu.VMEM((ROWS // 2, TILE, NB * TILE), bf16)] * 2
                + [pltpu.VMEM((ROWS // 2, NB * TILE, TILE), bf16)] * 2
            )
            * 2,
            pltpu.VMEM((faces_n, TILE, 2 * TILE), bf16),
            pltpu.VMEM((faces_n, TILE, 2 * TILE), bf16),
            pltpu.VMEM((4, ROWS, COLS, TILE), f32),
            pltpu.VMEM((ROWS, 2 * COLS, TILE), bf16),
            pltpu.VMEM((ROWS, COLS, TILE), f32),
            pltpu.VMEM((ROWS * COLS, TILE), f32),
            pltpu.VMEM((TERMS * COLS, TILE), f32),
            pltpu.VMEM((2, 2, FROWS, COLS, TILE), f32),
            pltpu.VMEM((2, 2, FROWS, COLS, TILE), f32),
            pltpu.VMEM((2, 2, FROWS, COLS, TILE), f32),
            pltpu.VMEM((2, 2, FROWS, COLS, TILE), f32),
            pltpu.VMEM((ROWS, 384), f32),
            pltpu.VMEM((ROWS, 2 * COLS, TILE), bf16),
            pltpu.VMEM((faces_n, 2 * COLS, TILE), bf16),
            pltpu.VMEM((COLS, 128), f32),
            pltpu.VMEM((gx, 8, 128), f32),
            pltpu.VMEM((gy, 8, 128), f32),
            pltpu.VMEM((gx, 8, 128), f32),
            pltpu.VMEM((gy, 8, 128), f32),
            pltpu.SemaphoreType.DMA((SLOTS,)),
            pltpu.SemaphoreType.DMA,
            pltpu.SemaphoreType.DMA,
            pltpu.SemaphoreType.DMA((6,)),
            pltpu.SemaphoreType.DMA,
            pltpu.SemaphoreType.DMA((2, 2)),
            pltpu.SemaphoreType.DMA((2, 2)),
            pltpu.SemaphoreType.DMA((2, 2)),
            pltpu.SemaphoreType.DMA((2, 2)),
            pltpu.SemaphoreType.DMA((2 * (gx + gy),)),
            pltpu.SemaphoreType.DMA((2 * (gx + gy),)),
        ],
        compiler_params=pltpu.CompilerParams(
            collective_id=0, has_side_effects=True, vmem_limit_bytes=62 << 20
        ),
    )(cols, rows, bounds, diag, start, tiles, faces)
    return pl.pallas_call(
        hand_over,
        out_shape=shapes,
        in_specs=[hbm] * 2,
        out_specs=(hbm, hbm),
        scratch_shapes=[
            pltpu.VMEM((ROWS, COLS, TILE), f32),
            pltpu.VMEM((COLS, COLS), f32),
            pltpu.SemaphoreType.DMA((2, ROWS // GROUP + 1)),
        ],
    )(*results)


def shards(start_block, tiles, tile_cols, node_diag, face_tiles, face_rows, filter_bounds):
    gx, gy = lax.axis_size("gx"), lax.axis_size("gy")
    basis, projected = run(
        gx, gy,
        tile_cols[0, 0].T, face_rows[0, 0], filter_bounds, node_diag[0, 0], start_block[0, 0],
        tiles[0, 0], face_tiles[0, 0].reshape(2 * FROWS, TILE, TILE),
    )
    return basis[None, None], projected


def solution(mesh):
    in_specs = (
        P("gx", "gy", None, None, None),
        P("gx", "gy", None, None, None, None),
        P("gx", "gy", None, None),
        P("gx", "gy", None, None),
        P("gx", "gy", None, None, None, None),
        P("gx", "gy", None, None),
        P(),
    )
    out_specs = (P("gx", "gy", None, None, None), P())
    return jax.shard_map(shards, mesh=mesh, in_specs=in_specs, out_specs=out_specs, check_vma=False)
```

```python
import functools

import jax
import jax.numpy as jnp
from jax import lax
from jax.experimental import pallas as pl
from jax.experimental.pallas import tpu as pltpu
from jax.sharding import PartitionSpec as P

MESH = pl.DeviceIdType.MESH
f32, bf16 = jnp.float32, jnp.bfloat16
NN = (((1,), (0,)), ((), ()))
NT = (((1,), (1,)), ((), ()))
ROWS, NB, COLS, TILE, FROWS = 64, 4, 16, 128, 24
GROUP = 8
NGROUPS = ROWS // GROUP
LOCAL = ROWS * NB
SLOTS = 4
INNER = 4
BIG = 16
TERMS = 336


def dot(a, b, dims=NN):
    return lax.dot_general(a, b, dims, preferred_element_type=f32)


def split(x):
    high = x.astype(bf16)
    return high, (x - high.astype(f32)).astype(bf16)


def stacked(x):
    return jnp.concatenate(split(x), axis=0)


def times(pair, high, low, dims=NN):
    both = dot(pair, high, dims)
    return both[:COLS] + both[COLS:] + dot(pair[:COLS], low, dims)


def times_wide(pair, both):
    out = dot(pair, both)
    out = out[:COLS] + out[COLS:]
    return out[:, :TILE] + out[:, TILE:]


def exact(a, b, dims):
    return lax.dot_general(
        a, b, dims, precision=lax.Precision.HIGHEST, preferred_element_type=f32
    )


def kernel(
    gx, gy,
    cols_h, rows_h, bounds_h, diag_h, start_h, tiles_h, faces_h,
    basis_h, proj,
    cols_s, rows_s, bounds_s, cols_v, rows_v, diag, stage, fstage,
    tn_h0, tn_l0, tt_h0, tt_l0, tn_h1, tn_l1, tt_h1, tt_l1, cn, ct,
    vb, vs, acc, scat, terms, low, down_s, down_r, up_s, hot, ys, fys,
    pad, gbuf0, gbuf1, gbuf2, sbuf0, sbuf1, sbuf2,
    stage_sem, fstage_sem, start_sem, small_sem, out_sem,
    down_ss, down_rs, up_ss, up_rs, red_ss, red_rs,
):
    u, v = lax.axis_index("gx"), lax.axis_index("gy")
    held = (tn_h0, tn_l0, tt_h0, tt_l0), (tn_h1, tn_l1, tt_h1, tt_l1)
    nodes = float(gx * gy * ROWS * TILE)

    def stage_copy(group):
        slot = lax.rem(group, SLOTS)
        return pltpu.make_async_copy(
            tiles_h.at[pl.ds(group * GROUP, GROUP)], stage.at[slot], stage_sem.at[slot]
        )

    pairs = (
        (cols_h, cols_v), (rows_h, rows_v), (rows_h, rows_s), (cols_h, cols_s),
        (bounds_h, bounds_s), (diag_h, diag),
    )
    small = [pltpu.make_async_copy(a, b, small_sem.at[n]) for n, (a, b) in enumerate(pairs)]
    for copy in small[:2]:
        copy.start()
    start_copy = pltpu.make_async_copy(start_h, vb.at[0], start_sem)
    start_copy.start()
    for copy in small[2:]:
        copy.start()
    face_copies = [
        pltpu.make_async_copy(
            faces_h.at[pl.ds(axis * FROWS, FROWS)],
            fstage.at[pl.ds(axis * FROWS, FROWS)],
            fstage_sem.at[axis],
        )
        for axis in range(2)
    ]
    face_copies[1].start()
    face_copies[0].start()

    lower = (lax.rem(u + gx - 1, gx), v), (u, lax.rem(v + gy - 1, gy))
    upper = (lax.rem(u + 1, gx), v), (u, lax.rem(v + 1, gy))

    outer = gy // INNER
    v_out, v_in = v // INNER, lax.rem(v, INNER)
    sums = (
        (gx, u, lambda step: (lax.rem(u + step, gx), v)),
        (INNER, v_in, lambda step: (u, v_out * INNER + lax.rem(v_in + step, INNER))),
        (outer, v_out, lambda step: (u, lax.rem(v + step * INNER, gy))),
    )
    barrier = pltpu.get_barrier_semaphore()
    greeted = [peer(step) for size, _, peer in sums for step in range(1, size)]
    greeted += [lower[1], upper[1]]
    for peer in greeted:
        pl.semaphore_signal(barrier, inc=1, device_id=peer, device_id_type=MESH)

    def down_copy(axis, slot):
        return pltpu.make_async_remote_copy(
            src_ref=down_s.at[slot, axis], dst_ref=down_r.at[slot, axis],
            send_sem=down_ss.at[slot, axis], recv_sem=down_rs.at[slot, axis],
            device_id=lower[axis], device_id_type=MESH,
        )

    def up_copy(axis, slot):
        return pltpu.make_async_remote_copy(
            src_ref=up_s.at[slot, axis], dst_ref=low.at[slot, axis],
            send_sem=up_ss.at[slot, axis], recv_sem=up_rs.at[slot, axis],
            device_id=upper[axis], device_id_type=MESH,
        )

    tall = lax.broadcasted_iota(jnp.int32, (ROWS, FROWS), 0)
    taller = lax.broadcasted_iota(jnp.int32, (ROWS, ROWS), 0)
    for copy in small:
        copy.wait()
    for k in range(NB):
        match = (cols_v[k : k + 1, :] == taller).astype(f32)
        hot[:, k * ROWS : (k + 1) * ROWS] = match
    hot[:, LOCAL:] = jnp.zeros((ROWS, 128), f32)
    has_upper = ((u < gx - 1).astype(f32), (v < gy - 1).astype(f32))
    has_lower = ((u > 0).astype(f32), (v > 0).astype(f32))
    for axis in range(2):
        gain = (rows_v[2 * axis : 2 * axis + 1, :] == tall).astype(f32) * has_upper[axis]
        hot[:, LOCAL + axis * FROWS : LOCAL + (axis + 1) * FROWS] = gain
        lost = (rows_v[2 * axis + 1 : 2 * axis + 2, :] == tall).astype(f32) * has_lower[axis]
        hot[:, TERMS + axis * FROWS : TERMS + (axis + 1) * FROWS] = lost
    terms[(LOCAL + 2 * FROWS) * COLS :, :] = jnp.zeros(
        ((TERMS - LOCAL - 2 * FROWS) * COLS, TILE), f32
    )
    pad[...] = jnp.zeros((COLS, 128), f32)

    low_end = jnp.full((COLS, TILE), bounds_s[0], f32)
    high_end = jnp.full((COLS, TILE), bounds_s[1], f32)
    inverse_half = 2.0 / (high_end - low_end)
    centre = (high_end + low_end) * 0.5

    start_copy.wait()

    def split_rows(i, _):
        vs[i] = stacked(vb[0, i])
        return 0

    lax.fori_loop(0, ROWS, split_rows, 0, unroll=8)

    def fill_down(k, slot):
        def one(j, _):
            for axis in range(2):
                down_s[slot, axis, j] = vb[k, rows_s[2 * axis + 1, j]]
            return 0

        lax.fori_loop(0, FROWS, one, 0, unroll=8)

    def products(slot, axis, first):
        def one(j, _):
            f = axis * FROWS + j
            if first:
                high, small = split(fstage[f])
                both = jnp.concatenate([high, small], axis=1)
                cn[f] = both
                ct[f, :, :TILE] = jnp.transpose(high)
                ct[f, :, TILE:] = jnp.transpose(small)
            else:
                both = cn[f]
            up_s[slot, axis, j] = times_wide(vs[rows_s[2 * axis, j]], both)
            return 0

        lax.fori_loop(0, FROWS, one, 0, unroll=True)

    def gather4(i):
        return jnp.concatenate([vs[cols_s[k, i]] for k in range(NB)], axis=1)

    def convert_row(part, t, slot, r):
        tn_h, tn_l, tt_h, tt_l = held[part]
        for k in range(NB):
            high, small = split(stage[slot, r, k])
            lanes = slice(k * TILE, (k + 1) * TILE)
            tn_h[t, :, lanes] = high
            tn_l[t, :, lanes] = small
            tt_h[t, lanes, :] = jnp.transpose(high)
            tt_l[t, lanes, :] = jnp.transpose(small)

    def full_row(part, t, i):
        tn_h, tn_l, tt_h, tt_l = held[part]
        acc[i] = times(gather4(i), tt_h[t], tt_l[t])
        back = times(vs[i], tn_h[t], tn_l[t])
        for k in range(NB):
            at = pl.multiple_of((k * ROWS + i) * COLS, COLS)
            terms[pl.ds(at, COLS), :] = back[:, k * TILE : (k + 1) * TILE]

    def gains(slot):
        def one(j, _):
            for axis in range(2):
                f = axis * FROWS + j
                at = pl.multiple_of((LOCAL + f) * COLS, COLS)
                terms[pl.ds(at, COLS), :] = times_wide(
                    stacked(down_r[slot, axis, j]), ct[f]
                )
            return 0

        lax.fori_loop(0, FROWS, one, 0, unroll=True)

    def scatter(slot):
        places = hot[...].astype(bf16)
        got = low.at[slot].reshape(2 * FROWS * COLS, TILE)
        for c in range(COLS):
            column = jnp.concatenate(
                [
                    terms[pl.ds(c, TERMS, stride=COLS), :],
                    got[pl.ds(c, 2 * FROWS, stride=COLS), :],
                ],
                axis=0,
            )
            out = dot(places, jnp.concatenate(split(column), axis=1))
            scat[pl.ds(c, ROWS, stride=COLS), :] = out[:, :TILE] + out[:, TILE:]

    def update(k, before, scale, keep):
        def one(i, _):
            block = vb[k, i]
            at = pl.multiple_of(i * COLS, COLS)
            applied = diag[pl.ds(i, 1), :] * block + acc[i] + scat[pl.ds(at, COLS), :]
            new = scale * (applied - centre * block)
            if keep:
                new = new - vb[before, i]
            vb[k + 1, i] = new
            vs[i] = stacked(new)
            return 0

        lax.fori_loop(0, ROWS, one, 0, unroll=8)

    def apply(k, first):
        slot = lax.rem(k, 2)
        fill_down(k, slot)
        if first:
            pl.semaphore_wait(barrier, len(greeted))
        down_copy(1, slot).start()
        down_copy(0, slot).start()
        for axis in (1, 0):
            if first:
                face_copies[axis].wait()
                if axis == 0:
                    for group in range(SLOTS):
                        stage_copy(group).start()
            products(slot, axis, first)
            up_copy(axis, slot).start()

        def convert_group(part, pair, r):
            convert_row(part, pair * GROUP + r, lax.rem(2 * pair + part, SLOTS), r)

        def full_group(part, pair, r):
            full_row(part, pair * GROUP + r, (2 * pair + part) * GROUP + r)

        if first:
            stage_copy(0).wait()
            for r in range(GROUP):
                convert_group(0, 0, r)

            def two_groups(pair, _):
                @pl.when(pair < NGROUPS // 2 - 2)
                def _():
                    stage_copy(2 * pair + 4).start()

                stage_copy(2 * pair + 1).wait()
                for r in range(GROUP):
                    convert_group(1, pair, r)
                    full_group(0, pair, r)

                @pl.when(pair < NGROUPS // 2 - 2)
                def _():
                    stage_copy(2 * pair + 5).start()

                stage_copy(2 * pair + 2).wait()
                for r in range(GROUP):
                    convert_group(0, pair + 1, r)
                    full_group(1, pair, r)
                return 0

            lax.fori_loop(0, NGROUPS // 2 - 1, two_groups, 0)
            last = NGROUPS // 2 - 1
            stage_copy(NGROUPS - 1).wait()
            for r in range(GROUP):
                convert_group(1, last, r)
                full_group(0, last, r)
            for r in range(GROUP):
                full_group(1, last, r)
        else:

            def plain(pair, _):
                for part in range(2):
                    for r in range(GROUP):
                        full_group(part, pair, r)
                return 0

            lax.fori_loop(0, NGROUPS // 2, plain, 0)
        for axis in range(2):
            down_copy(axis, slot).wait()
        gains(slot)
        for axis in range(2):
            up_copy(axis, slot).wait()
        scatter(slot)

    apply(0, True)
    update(0, 0, inverse_half, False)

    def later(k, _):
        apply(k, False)
        update(k, k - 1, 2.0 * inverse_half, True)
        return 0

    lax.fori_loop(1, 3, later, 0)

    def pack(x):
        pad[:, 0 : 2 * COLS] = x[:COLS] + x[COLS:]
        full = pad[...]
        full = jnp.where(at < COLS, full + pltpu.roll(full, 128 - COLS, 1), 0.0)
        return full[:8] + pltpu.roll(full[8:], 64, 1)

    lanes = lax.broadcasted_iota(jnp.int32, (8, 128), 1)
    at = lax.broadcasted_iota(jnp.int32, (COLS, 128), 1)

    def unpack(p):
        top = jnp.where(lanes < COLS, p, 0.0)
        bottom = jnp.where(lanes < COLS, pltpu.roll(p, 64, 1), 0.0)
        return jnp.concatenate([top, bottom], axis=0)

    buffers = (gbuf0, gbuf1, gbuf2), (sbuf0, sbuf1, sbuf2)

    def reduce_copy(which, stage_no, step):
        size, _, peer = sums[stage_no]
        buffer = buffers[which][stage_no]
        at_sem = (which * 3 + stage_no) * gx + step
        return pltpu.make_async_remote_copy(
            src_ref=buffer.at[0], dst_ref=buffer.at[step],
            send_sem=red_ss.at[at_sem], recv_sem=red_rs.at[at_sem],
            device_id=peer(step), device_id_type=MESH,
        )

    def reduce_start(which, stage_no, value):
        buffers[which][stage_no][0] = value
        for step in range(1, sums[stage_no][0]):
            reduce_copy(which, stage_no, step).start()

    def reduce_end(which, stage_no):
        size, me, _ = sums[stage_no]
        buffer = buffers[which][stage_no]
        for step in range(1, size):
            reduce_copy(which, stage_no, step).wait()
        total = buffer[me]
        for source in range(1, size):
            total = total + buffer[lax.rem(me + size - source, size)]
        return total

    def inner(count, left, right):
        total = jnp.zeros((2 * COLS, 2 * COLS), f32)
        for g in range(count // BIG):
            a = jnp.concatenate([left(g * BIG + r) for r in range(BIG)], axis=1)
            b = jnp.concatenate([right(g * BIG + r) for r in range(BIG)], axis=1)
            total = total + dot(a, b, NT)
        return total

    fill_down(3, 1)
    down_copy(1, 1).start()
    down_copy(0, 1).start()
    gram = inner(ROWS, lambda i: vs[i], lambda i: vs[i])
    reduce_start(0, 0, pack(gram))

    def half_groups(pair, _):
        for part in range(2):
            high, small = held[part][2:]
            for r in range(GROUP):
                i = (2 * pair + part) * GROUP + r
                t = pair * GROUP + r
                image = times(gather4(i), high[t], small[t])
                image = image + 0.5 * (diag[pl.ds(i, 1), :] * vb[3, i])
                ys[i] = stacked(image)
        return 0

    lax.fori_loop(0, NGROUPS // 4, half_groups, 0)
    reduce_start(0, 1, reduce_end(0, 0))
    lax.fori_loop(NGROUPS // 4, NGROUPS // 2, half_groups, 0)
    reduce_start(0, 2, reduce_end(0, 1))
    for axis in range(2):
        down_copy(axis, 1).wait()

    def half_face(j, _):
        for axis in range(2):
            f = axis * FROWS + j
            image = times_wide(stacked(down_r[1, axis, j]), ct[f])
            fys[f] = stacked(image * has_upper[axis])
        return 0

    lax.fori_loop(0, FROWS, half_face, 0, unroll=True)
    half = inner(ROWS, lambda i: vs[i], lambda i: ys[i])
    half = half + inner(
        2 * FROWS, lambda f: vs[rows_s[2 * (f // FROWS), f % FROWS]], lambda f: fys[f]
    )
    reduce_start(1, 0, pack(half))

    work = unpack(reduce_end(0, 2)) * (1.0 / nodes)
    down = lax.broadcasted_iota(jnp.int32, (COLS, 128), 0)
    work = work + (at == down + 64).astype(f32)
    for j in range(COLS):
        if j == COLS // 2:
            reduce_start(1, 1, reduce_end(1, 0))
        pivot = work[j : j + 1, :]
        root = 1.0 / jnp.sqrt(pivot[:, j : j + 1])
        pivot = pivot * root
        factor = work[:, j : j + 1] * root
        work = jnp.where(down > j, work - factor * pivot, jnp.where(down == j, pivot, work))
    inverse = jnp.where(at < COLS, pltpu.roll(work, 64, 1), 0.0)
    high, small = split(inverse)
    twice = high.astype(f32)
    twice = twice + pltpu.roll(twice, COLS, 1)
    mixer = jnp.concatenate([twice.astype(bf16), small], axis=0)[:, : 2 * COLS]

    reduce_start(1, 2, reduce_end(1, 1))

    for g in range(ROWS // 4):
        four = jnp.concatenate([vs[g * 4 + r] for r in range(4)], axis=1)
        out = dot(mixer, four)
        out = out[:COLS] + out[COLS:]
        for r in range(4):
            vb[0, g * 4 + r] = out[:, r * TILE : (r + 1) * TILE]
    out_copy = pltpu.make_async_copy(vb.at[0], basis_h, out_sem)
    out_copy.start()

    summed = unpack(reduce_end(1, 2))[:, :COLS] * (1.0 / nodes)
    narrow = inverse[:, :COLS]
    both = exact(narrow, summed, NN) + exact(narrow, summed, NT)
    proj[...] = exact(both, narrow, NT)
    out_copy.wait()


def hand_over(basis_in, proj_in, basis, proj, held, small, sems):
    parts = ROWS // GROUP
    ins = [
        pltpu.make_async_copy(
            basis_in.at[pl.ds(g * GROUP, GROUP)], held.at[pl.ds(g * GROUP, GROUP)], sems.at[0, g]
        )
        for g in range(parts)
    ] + [pltpu.make_async_copy(proj_in, small, sems.at[0, parts])]
    outs = [
        pltpu.make_async_copy(
            held.at[pl.ds(g * GROUP, GROUP)], basis.at[pl.ds(g * GROUP, GROUP)], sems.at[1, g]
        )
        for g in range(parts)
    ] + [pltpu.make_async_copy(small, proj, sems.at[1, parts])]
    for copy in ins:
        copy.start()
    for first, second in zip(ins, outs):
        first.wait()
        second.start()
    for copy in outs:
        copy.wait()


def run(gx, gy, cols, rows, bounds, diag, start, tiles, faces):
    hbm = pl.BlockSpec(memory_space=pl.ANY)
    vmem = pl.BlockSpec(memory_space=pltpu.VMEM)
    faces_n = 2 * FROWS
    shapes = (
        jax.ShapeDtypeStruct((ROWS, COLS, TILE), f32),
        jax.ShapeDtypeStruct((COLS, COLS), f32),
    )
    results = pl.pallas_call(
        functools.partial(kernel, gx, gy),
        out_shape=shapes,
        in_specs=[hbm] * 7,
        out_specs=(hbm, vmem),
        scratch_shapes=[
            pltpu.SMEM((NB, ROWS), jnp.int32),
            pltpu.SMEM((4, FROWS), jnp.int32),
            pltpu.SMEM((2,), f32),
            pltpu.VMEM((NB, ROWS), jnp.int32),
            pltpu.VMEM((4, FROWS), jnp.int32),
            pltpu.VMEM((ROWS, TILE), f32),
            pltpu.VMEM((SLOTS, GROUP, NB, TILE, TILE), f32),
            pltpu.VMEM((faces_n, TILE, TILE), f32),
            *(
                [pltpu.VMEM((ROWS // 2, TILE, NB * TILE), bf16)] * 2
                + [pltpu.VMEM((ROWS // 2, NB * TILE, TILE), bf16)] * 2
            )
            * 2,
            pltpu.VMEM((faces_n, TILE, 2 * TILE), bf16),
            pltpu.VMEM((faces_n, TILE, 2 * TILE), bf16),
            pltpu.VMEM((4, ROWS, COLS, TILE), f32),
            pltpu.VMEM((ROWS, 2 * COLS, TILE), bf16),
            pltpu.VMEM((ROWS, COLS, TILE), f32),
            pltpu.VMEM((ROWS * COLS, TILE), f32),
            pltpu.VMEM((TERMS * COLS, TILE), f32),
            pltpu.VMEM((2, 2, FROWS, COLS, TILE), f32),
            pltpu.VMEM((2, 2, FROWS, COLS, TILE), f32),
            pltpu.VMEM((2, 2, FROWS, COLS, TILE), f32),
            pltpu.VMEM((2, 2, FROWS, COLS, TILE), f32),
            pltpu.VMEM((ROWS, 384), f32),
            pltpu.VMEM((ROWS, 2 * COLS, TILE), bf16),
            pltpu.VMEM((faces_n, 2 * COLS, TILE), bf16),
            pltpu.VMEM((COLS, 128), f32),
            *(
                pltpu.VMEM((gx, 8, 128), f32),
                pltpu.VMEM((INNER, 8, 128), f32),
                pltpu.VMEM((gy // INNER, 8, 128), f32),
            )
            * 2,
            pltpu.SemaphoreType.DMA((SLOTS,)),
            pltpu.SemaphoreType.DMA((2,)),
            pltpu.SemaphoreType.DMA,
            pltpu.SemaphoreType.DMA((6,)),
            pltpu.SemaphoreType.DMA,
            pltpu.SemaphoreType.DMA((2, 2)),
            pltpu.SemaphoreType.DMA((2, 2)),
            pltpu.SemaphoreType.DMA((2, 2)),
            pltpu.SemaphoreType.DMA((2, 2)),
            pltpu.SemaphoreType.DMA((6 * gx,)),
            pltpu.SemaphoreType.DMA((6 * gx,)),
        ],
        compiler_params=pltpu.CompilerParams(
            collective_id=0, has_side_effects=True, vmem_limit_bytes=62 << 20
        ),
    )(cols, rows, bounds, diag, start, tiles, faces)
    return pl.pallas_call(
        hand_over,
        out_shape=shapes,
        in_specs=[hbm] * 2,
        out_specs=(hbm, hbm),
        scratch_shapes=[
            pltpu.VMEM((ROWS, COLS, TILE), f32),
            pltpu.VMEM((COLS, COLS), f32),
            pltpu.SemaphoreType.DMA((2, ROWS // GROUP + 1)),
        ],
    )(*results)


def shards(start_block, tiles, tile_cols, node_diag, face_tiles, face_rows, filter_bounds):
    gx, gy = lax.axis_size("gx"), lax.axis_size("gy")
    basis, projected = run(
        gx, gy,
        tile_cols[0, 0].T, face_rows[0, 0], filter_bounds, node_diag[0, 0], start_block[0, 0],
        tiles[0, 0], face_tiles[0, 0].reshape(2 * FROWS, TILE, TILE),
    )
    return basis[None, None], projected


def solution(mesh):
    in_specs = (
        P("gx", "gy", None, None, None),
        P("gx", "gy", None, None, None, None),
        P("gx", "gy", None, None),
        P("gx", "gy", None, None),
        P("gx", "gy", None, None, None, None),
        P("gx", "gy", None, None),
        P(),
    )
    out_specs = (P("gx", "gy", None, None, None), P())
    return jax.shard_map(shards, mesh=mesh, in_specs=in_specs, out_specs=out_specs, check_vma=False)
```

```python
import functools

import jax
import jax.numpy as jnp
from jax import lax
from jax.experimental import pallas as pl
from jax.experimental.pallas import tpu as pltpu
from jax.sharding import PartitionSpec as P

MESH = pl.DeviceIdType.MESH
f32, bf16 = jnp.float32, jnp.bfloat16
NN = (((1,), (0,)), ((), ()))
NT = (((1,), (1,)), ((), ()))
ROWS, NB, COLS, TILE, FROWS = 64, 4, 16, 128, 24
GROUP = 8
NGROUPS = ROWS // GROUP
LOCAL = ROWS * NB
SLOTS = 4
BIG = 16
TERMS = 336


def dot(a, b, dims=NN):
    return lax.dot_general(a, b, dims, preferred_element_type=f32)


def split(x):
    high = x.astype(bf16)
    return high, (x - high.astype(f32)).astype(bf16)


def stacked(x):
    return jnp.concatenate(split(x), axis=0)


def times(pair, high, low, dims=NN):
    both = dot(pair, high, dims)
    return both[:COLS] + both[COLS:] + dot(pair[:COLS], low, dims)


def times_wide(pair, both):
    out = dot(pair, both)
    out = out[:COLS] + out[COLS:]
    return out[:, :TILE] + out[:, TILE:]


def exact(a, b, dims):
    return lax.dot_general(
        a, b, dims, precision=lax.Precision.HIGHEST, preferred_element_type=f32
    )


def kernel(
    gx, gy,
    cols_h, rows_h, bounds_h, diag_h, start_h, tiles_h, faces_h,
    basis_h, proj,
    cols_s, rows_s, bounds_s, cols_v, rows_v, diag, stage, fstage,
    tn_h0, tn_l0, tt_h0, tt_l0, tn_h1, tn_l1, tt_h1, tt_l1, cn, ct,
    vb, vs, acc, scat, terms, low, down_s, down_r, up_s, hot, ys, fys,
    pad, gbuf0, gbuf1, sbuf0, sbuf1,
    stage_sem, fstage_sem, start_sem, small_sem, out_sem,
    down_ss, down_rs, up_ss, up_rs, red_ss, red_rs,
):
    u, v = lax.axis_index("gx"), lax.axis_index("gy")
    held = (tn_h0, tn_l0, tt_h0, tt_l0), (tn_h1, tn_l1, tt_h1, tt_l1)
    nodes = float(gx * gy * ROWS * TILE)

    def stage_copy(group):
        slot = lax.rem(group, SLOTS)
        return pltpu.make_async_copy(
            tiles_h.at[pl.ds(group * GROUP, GROUP)], stage.at[slot], stage_sem.at[slot]
        )

    pairs = (
        (cols_h, cols_v), (rows_h, rows_v), (rows_h, rows_s), (cols_h, cols_s),
        (bounds_h, bounds_s), (diag_h, diag),
    )
    small = [pltpu.make_async_copy(a, b, small_sem.at[n]) for n, (a, b) in enumerate(pairs)]
    for copy in small[:2]:
        copy.start()
    start_copy = pltpu.make_async_copy(start_h, vb.at[0], start_sem)
    start_copy.start()
    for copy in small[2:]:
        copy.start()
    face_copies = [
        pltpu.make_async_copy(
            faces_h.at[pl.ds(axis * FROWS, FROWS)],
            fstage.at[pl.ds(axis * FROWS, FROWS)],
            fstage_sem.at[axis],
        )
        for axis in range(2)
    ]
    face_copies[1].start()
    face_copies[0].start()

    def past(me, step, size):
        other = me + step
        return jnp.where(other >= size, other - size, other)

    sums = (
        (gx, u, [(past(u, step, gx), v) for step in range(1, gx)]),
        (gy, v, [(u, past(v, step, gy)) for step in range(1, gy)]),
    )
    lower = sums[0][2][gx - 2], sums[1][2][gy - 2]
    upper = sums[0][2][0], sums[1][2][0]
    barrier = pltpu.get_barrier_semaphore()
    greeted = sums[0][2] + sums[1][2]
    for peer in greeted:
        pl.semaphore_signal(barrier, inc=1, device_id=peer, device_id_type=MESH)

    def down_copy(axis, slot):
        return pltpu.make_async_remote_copy(
            src_ref=down_s.at[slot, axis], dst_ref=down_r.at[slot, axis],
            send_sem=down_ss.at[slot, axis], recv_sem=down_rs.at[slot, axis],
            device_id=lower[axis], device_id_type=MESH,
        )

    def up_copy(axis, slot):
        return pltpu.make_async_remote_copy(
            src_ref=up_s.at[slot, axis], dst_ref=low.at[slot, axis],
            send_sem=up_ss.at[slot, axis], recv_sem=up_rs.at[slot, axis],
            device_id=upper[axis], device_id_type=MESH,
        )

    tall = lax.broadcasted_iota(jnp.int32, (ROWS, FROWS), 0)
    taller = lax.broadcasted_iota(jnp.int32, (ROWS, ROWS), 0)
    for copy in small:
        copy.wait()
    for k in range(NB):
        match = (cols_v[k : k + 1, :] == taller).astype(f32)
        hot[:, k * ROWS : (k + 1) * ROWS] = match
    hot[:, LOCAL:] = jnp.zeros((ROWS, 128), f32)
    has_upper = ((u < gx - 1).astype(f32), (v < gy - 1).astype(f32))
    has_lower = ((u > 0).astype(f32), (v > 0).astype(f32))
    for axis in range(2):
        gain = (rows_v[2 * axis : 2 * axis + 1, :] == tall).astype(f32) * has_upper[axis]
        hot[:, LOCAL + axis * FROWS : LOCAL + (axis + 1) * FROWS] = gain
        lost = (rows_v[2 * axis + 1 : 2 * axis + 2, :] == tall).astype(f32) * has_lower[axis]
        hot[:, TERMS + axis * FROWS : TERMS + (axis + 1) * FROWS] = lost
    terms[(LOCAL + 2 * FROWS) * COLS :, :] = jnp.zeros(
        ((TERMS - LOCAL - 2 * FROWS) * COLS, TILE), f32
    )
    pad[...] = jnp.zeros((COLS, 128), f32)

    low_end = jnp.full((COLS, TILE), bounds_s[0], f32)
    high_end = jnp.full((COLS, TILE), bounds_s[1], f32)
    inverse_half = 2.0 / (high_end - low_end)
    centre = (high_end + low_end) * 0.5

    start_copy.wait()

    def split_rows(i, _):
        vs[i] = stacked(vb[0, i])
        return 0

    lax.fori_loop(0, ROWS, split_rows, 0, unroll=8)

    def fill_down(k, slot):
        def one(j, _):
            for axis in range(2):
                down_s[slot, axis, j] = vb[k, rows_s[2 * axis + 1, j]]
            return 0

        lax.fori_loop(0, FROWS, one, 0, unroll=8)

    def products(slot, axis, first):
        def one(j, _):
            f = axis * FROWS + j
            if first:
                high, small = split(fstage[f])
                both = jnp.concatenate([high, small], axis=1)
                cn[f] = both
                ct[f, :, :TILE] = jnp.transpose(high)
                ct[f, :, TILE:] = jnp.transpose(small)
            else:
                both = cn[f]
            up_s[slot, axis, j] = times_wide(vs[rows_s[2 * axis, j]], both)
            return 0

        lax.fori_loop(0, FROWS, one, 0, unroll=True)

    def gather4(i):
        return jnp.concatenate([vs[cols_s[k, i]] for k in range(NB)], axis=1)

    def convert_row(part, t, slot, r):
        tn_h, tn_l, tt_h, tt_l = held[part]
        for k in range(NB):
            high, small = split(stage[slot, r, k])
            lanes = slice(k * TILE, (k + 1) * TILE)
            tn_h[t, :, lanes] = high
            tn_l[t, :, lanes] = small
            tt_h[t, lanes, :] = jnp.transpose(high)
            tt_l[t, lanes, :] = jnp.transpose(small)

    def full_row(part, t, i):
        tn_h, tn_l, tt_h, tt_l = held[part]
        acc[i] = times(gather4(i), tt_h[t], tt_l[t])
        back = times(vs[i], tn_h[t], tn_l[t])
        for k in range(NB):
            at = pl.multiple_of((k * ROWS + i) * COLS, COLS)
            terms[pl.ds(at, COLS), :] = back[:, k * TILE : (k + 1) * TILE]

    def gains(slot):
        def one(j, _):
            for axis in range(2):
                f = axis * FROWS + j
                at = pl.multiple_of((LOCAL + f) * COLS, COLS)
                terms[pl.ds(at, COLS), :] = times_wide(
                    stacked(down_r[slot, axis, j]), ct[f]
                )
            return 0

        lax.fori_loop(0, FROWS, one, 0, unroll=True)

    def scatter(slot):
        places = hot[...].astype(bf16)
        got = low.at[slot].reshape(2 * FROWS * COLS, TILE)
        for c in range(COLS):
            column = jnp.concatenate(
                [
                    terms[pl.ds(c, TERMS, stride=COLS), :],
                    got[pl.ds(c, 2 * FROWS, stride=COLS), :],
                ],
                axis=0,
            )
            out = dot(places, jnp.concatenate(split(column), axis=1))
            scat[pl.ds(c, ROWS, stride=COLS), :] = out[:, :TILE] + out[:, TILE:]

    def update(k, before, scale, keep):
        def one(i, _):
            block = vb[k, i]
            at = pl.multiple_of(i * COLS, COLS)
            applied = diag[pl.ds(i, 1), :] * block + acc[i] + scat[pl.ds(at, COLS), :]
            new = scale * (applied - centre * block)
            if keep:
                new = new - vb[before, i]
            vb[k + 1, i] = new
            vs[i] = stacked(new)
            return 0

        lax.fori_loop(0, ROWS, one, 0, unroll=8)

    def apply(k, first):
        slot = lax.rem(k, 2)
        fill_down(k, slot)
        if first:
            pl.semaphore_wait(barrier, len(greeted))
        down_copy(1, slot).start()
        down_copy(0, slot).start()
        for axis in (1, 0):
            if first:
                face_copies[axis].wait()
                if axis == 1:
                    for group in range(SLOTS):
                        stage_copy(group).start()
            products(slot, axis, first)
            up_copy(axis, slot).start()

        def convert_group(part, pair, r):
            convert_row(part, pair * GROUP + r, lax.rem(2 * pair + part, SLOTS), r)

        def full_group(part, pair, r):
            full_row(part, pair * GROUP + r, (2 * pair + part) * GROUP + r)

        if first:
            stage_copy(0).wait()
            for r in range(GROUP):
                convert_group(0, 0, r)

            def two_groups(pair, _):
                @pl.when(pair < NGROUPS // 2 - 2)
                def _():
                    stage_copy(2 * pair + 4).start()

                stage_copy(2 * pair + 1).wait()
                for r in range(GROUP):
                    convert_group(1, pair, r)
                    full_group(0, pair, r)

                @pl.when(pair < NGROUPS // 2 - 2)
                def _():
                    stage_copy(2 * pair + 5).start()

                stage_copy(2 * pair + 2).wait()
                for r in range(GROUP):
                    convert_group(0, pair + 1, r)
                    full_group(1, pair, r)
                return 0

            lax.fori_loop(0, NGROUPS // 2 - 1, two_groups, 0)
            last = NGROUPS // 2 - 1
            stage_copy(NGROUPS - 1).wait()
            for r in range(GROUP):
                convert_group(1, last, r)
                full_group(0, last, r)
            for r in range(GROUP):
                full_group(1, last, r)
        else:

            def plain(pair, _):
                for part in range(2):
                    for r in range(GROUP):
                        full_group(part, pair, r)
                return 0

            lax.fori_loop(0, NGROUPS // 2, plain, 0)
        for axis in range(2):
            down_copy(axis, slot).wait()
        gains(slot)
        for axis in range(2):
            up_copy(axis, slot).wait()
        scatter(slot)

    apply(0, True)
    update(0, 0, inverse_half, False)

    def later(k, _):
        apply(k, False)
        update(k, k - 1, 2.0 * inverse_half, True)
        return 0

    lax.fori_loop(1, 3, later, 0)

    def pack(x):
        pad[:, 0 : 2 * COLS] = x[:COLS] + x[COLS:]
        full = pad[...]
        full = jnp.where(at < COLS, full + pltpu.roll(full, 128 - COLS, 1), 0.0)
        return full[:8] + pltpu.roll(full[8:], 64, 1)

    lanes = lax.broadcasted_iota(jnp.int32, (8, 128), 1)
    at = lax.broadcasted_iota(jnp.int32, (COLS, 128), 1)

    def unpack(p):
        top = jnp.where(lanes < COLS, p, 0.0)
        bottom = jnp.where(lanes < COLS, pltpu.roll(p, 64, 1), 0.0)
        return jnp.concatenate([top, bottom], axis=0)

    buffers = (gbuf0, gbuf1), (sbuf0, sbuf1)

    def reduce_copies(which, stage_no):
        _, me, peers = sums[stage_no]
        own = buffers[which][stage_no].at[me]
        base = (which * 2 + stage_no) * gy
        return [
            pltpu.make_async_remote_copy(
                src_ref=own, dst_ref=own,
                send_sem=red_ss.at[base + n], recv_sem=red_rs.at[base + n],
                device_id=peer, device_id_type=MESH,
            )
            for n, peer in enumerate(peers)
        ]

    def reduce_start(which, stage_no, value):
        buffers[which][stage_no][sums[stage_no][1]] = value
        for copy in reduce_copies(which, stage_no):
            copy.start()

    def reduce_end(which, stage_no):
        size = sums[stage_no][0]
        copies = reduce_copies(which, stage_no)
        for copy in copies:
            copy.wait_send()
        for copy in copies:
            copy.wait_recv()
        parts = [buffers[which][stage_no][source] for source in range(size)]
        while len(parts) > 1:
            parts = [a + b for a, b in zip(parts[0::2], parts[1::2])]
        return parts[0]

    def inner(count, left, right):
        total = jnp.zeros((2 * COLS, 2 * COLS), f32)
        for g in range(count // BIG):
            a = jnp.concatenate([left(g * BIG + r) for r in range(BIG)], axis=1)
            b = jnp.concatenate([right(g * BIG + r) for r in range(BIG)], axis=1)
            total = total + dot(a, b, NT)
        return total

    fill_down(3, 1)
    down_copy(1, 1).start()
    down_copy(0, 1).start()
    gram = inner(ROWS, lambda i: vs[i], lambda i: vs[i])
    reduce_start(0, 0, pack(gram))

    def half_groups(pair, _):
        for part in range(2):
            high, small = held[part][2:]
            for r in range(GROUP):
                i = (2 * pair + part) * GROUP + r
                t = pair * GROUP + r
                image = times(gather4(i), high[t], small[t])
                image = image + 0.5 * (diag[pl.ds(i, 1), :] * vb[3, i])
                ys[i] = stacked(image)
        return 0

    lax.fori_loop(0, NGROUPS // 4, half_groups, 0)
    reduce_start(0, 1, reduce_end(0, 0))
    lax.fori_loop(NGROUPS // 4, NGROUPS // 2, half_groups, 0)
    for axis in range(2):
        down_copy(axis, 1).wait()

    def half_face(j, _):
        for axis in range(2):
            f = axis * FROWS + j
            image = times_wide(stacked(down_r[1, axis, j]), ct[f])
            fys[f] = stacked(image * has_upper[axis])
        return 0

    lax.fori_loop(0, FROWS, half_face, 0, unroll=True)
    half = inner(ROWS, lambda i: vs[i], lambda i: ys[i])
    half = half + inner(
        2 * FROWS, lambda f: vs[rows_s[2 * (f // FROWS), f % FROWS]], lambda f: fys[f]
    )
    reduce_start(1, 0, pack(half))

    work = unpack(reduce_end(0, 1)) * (1.0 / nodes)
    down = lax.broadcasted_iota(jnp.int32, (COLS, 128), 0)
    work = work + (at == down + 64).astype(f32)
    for j in range(COLS):
        pivot = work[j : j + 1, :]
        root = 1.0 / jnp.sqrt(pivot[:, j : j + 1])
        pivot = pivot * root
        factor = work[:, j : j + 1] * root
        work = jnp.where(down > j, work - factor * pivot, jnp.where(down == j, pivot, work))
    inverse = jnp.where(at < COLS, pltpu.roll(work, 64, 1), 0.0)
    high, small = split(inverse)
    twice = high.astype(f32)
    twice = twice + pltpu.roll(twice, COLS, 1)
    mixer = jnp.concatenate([twice.astype(bf16), small], axis=0)[:, : 2 * COLS]

    reduce_start(1, 1, reduce_end(1, 0))

    for g in range(ROWS // 4):
        four = jnp.concatenate([vs[g * 4 + r] for r in range(4)], axis=1)
        out = dot(mixer, four)
        out = out[:COLS] + out[COLS:]
        for r in range(4):
            vb[0, g * 4 + r] = out[:, r * TILE : (r + 1) * TILE]
    out_copy = pltpu.make_async_copy(vb.at[0], basis_h, out_sem)
    out_copy.start()

    summed = unpack(reduce_end(1, 1))[:, :COLS] * (1.0 / nodes)
    narrow = inverse[:, :COLS]
    both = exact(narrow, summed, NN) + exact(narrow, summed, NT)
    proj[...] = exact(both, narrow, NT)
    out_copy.wait()


def hand_over(basis_in, proj_in, basis, proj, held, small, sems):
    parts = ROWS // GROUP
    ins = [
        pltpu.make_async_copy(
            basis_in.at[pl.ds(g * GROUP, GROUP)], held.at[pl.ds(g * GROUP, GROUP)], sems.at[0, g]
        )
        for g in range(parts)
    ] + [pltpu.make_async_copy(proj_in, small, sems.at[0, parts])]
    outs = [
        pltpu.make_async_copy(
            held.at[pl.ds(g * GROUP, GROUP)], basis.at[pl.ds(g * GROUP, GROUP)], sems.at[1, g]
        )
        for g in range(parts)
    ] + [pltpu.make_async_copy(small, proj, sems.at[1, parts])]
    for copy in ins:
        copy.start()
    for first, second in zip(ins, outs):
        first.wait()
        second.start()
    for copy in outs:
        copy.wait()


def run(gx, gy, cols, rows, bounds, diag, start, tiles, faces):
    hbm = pl.BlockSpec(memory_space=pl.ANY)
    vmem = pl.BlockSpec(memory_space=pltpu.VMEM)
    faces_n = 2 * FROWS
    shapes = (
        jax.ShapeDtypeStruct((ROWS, COLS, TILE), f32),
        jax.ShapeDtypeStruct((COLS, COLS), f32),
    )
    results = pl.pallas_call(
        functools.partial(kernel, gx, gy),
        out_shape=shapes,
        in_specs=[hbm] * 7,
        out_specs=(hbm, vmem),
        scratch_shapes=[
            pltpu.SMEM((NB, ROWS), jnp.int32),
            pltpu.SMEM((4, FROWS), jnp.int32),
            pltpu.SMEM((2,), f32),
            pltpu.VMEM((NB, ROWS), jnp.int32),
            pltpu.VMEM((4, FROWS), jnp.int32),
            pltpu.VMEM((ROWS, TILE), f32),
            pltpu.VMEM((SLOTS, GROUP, NB, TILE, TILE), f32),
            pltpu.VMEM((faces_n, TILE, TILE), f32),
            *(
                [pltpu.VMEM((ROWS // 2, TILE, NB * TILE), bf16)] * 2
                + [pltpu.VMEM((ROWS // 2, NB * TILE, TILE), bf16)] * 2
            )
            * 2,
            pltpu.VMEM((faces_n, TILE, 2 * TILE), bf16),
            pltpu.VMEM((faces_n, TILE, 2 * TILE), bf16),
            pltpu.VMEM((4, ROWS, COLS, TILE), f32),
            pltpu.VMEM((ROWS, 2 * COLS, TILE), bf16),
            pltpu.VMEM((ROWS, COLS, TILE), f32),
            pltpu.VMEM((ROWS * COLS, TILE), f32),
            pltpu.VMEM((TERMS * COLS, TILE), f32),
            pltpu.VMEM((2, 2, FROWS, COLS, TILE), f32),
            pltpu.VMEM((2, 2, FROWS, COLS, TILE), f32),
            pltpu.VMEM((2, 2, FROWS, COLS, TILE), f32),
            pltpu.VMEM((2, 2, FROWS, COLS, TILE), f32),
            pltpu.VMEM((ROWS, 384), f32),
            pltpu.VMEM((ROWS, 2 * COLS, TILE), bf16),
            pltpu.VMEM((faces_n, 2 * COLS, TILE), bf16),
            pltpu.VMEM((COLS, 128), f32),
            *(
                pltpu.VMEM((gx, 8, 128), f32),
                pltpu.VMEM((gy, 8, 128), f32),
            )
            * 2,
            pltpu.SemaphoreType.DMA((SLOTS,)),
            pltpu.SemaphoreType.DMA((2,)),
            pltpu.SemaphoreType.DMA,
            pltpu.SemaphoreType.DMA((6,)),
            pltpu.SemaphoreType.DMA,
            pltpu.SemaphoreType.DMA((2, 2)),
            pltpu.SemaphoreType.DMA((2, 2)),
            pltpu.SemaphoreType.DMA((2, 2)),
            pltpu.SemaphoreType.DMA((2, 2)),
            pltpu.SemaphoreType.DMA((4 * gy,)),
            pltpu.SemaphoreType.DMA((4 * gy,)),
        ],
        compiler_params=pltpu.CompilerParams(
            collective_id=0, has_side_effects=True, vmem_limit_bytes=62 << 20
        ),
    )(cols, rows, bounds, diag, start, tiles, faces)
    return pl.pallas_call(
        hand_over,
        out_shape=shapes,
        in_specs=[hbm] * 2,
        out_specs=(hbm, hbm),
        scratch_shapes=[
            pltpu.VMEM((ROWS, COLS, TILE), f32),
            pltpu.VMEM((COLS, COLS), f32),
            pltpu.SemaphoreType.DMA((2, ROWS // GROUP + 1)),
        ],
    )(*results)


def shards(start_block, tiles, tile_cols, node_diag, face_tiles, face_rows, filter_bounds):
    gx, gy = lax.axis_size("gx"), lax.axis_size("gy")
    basis, projected = run(
        gx, gy,
        tile_cols[0, 0].T, face_rows[0, 0], filter_bounds, node_diag[0, 0], start_block[0, 0],
        tiles[0, 0], face_tiles[0, 0].reshape(2 * FROWS, TILE, TILE),
    )
    return basis[None, None], projected


def solution(mesh):
    in_specs = (
        P("gx", "gy", None, None, None),
        P("gx", "gy", None, None, None, None),
        P("gx", "gy", None, None),
        P("gx", "gy", None, None),
        P("gx", "gy", None, None, None, None),
        P("gx", "gy", None, None),
        P(),
    )
    out_specs = (P("gx", "gy", None, None, None), P())
    return jax.shard_map(shards, mesh=mesh, in_specs=in_specs, out_specs=out_specs, check_vma=False)
```

```python
import functools

import jax
import jax.numpy as jnp
from jax import lax
from jax.experimental import pallas as pl
from jax.experimental.pallas import tpu as pltpu
from jax.sharding import PartitionSpec as P

MESH = pl.DeviceIdType.MESH
f32, bf16 = jnp.float32, jnp.bfloat16
NN = (((1,), (0,)), ((), ()))
NT = (((1,), (1,)), ((), ()))
ROWS, NB, COLS, TILE, FROWS = 64, 4, 16, 128, 24
GROUP = 8
NGROUPS = ROWS // GROUP
LOCAL = ROWS * NB
SLOTS = 4
BIG = 16
TERMS = 336


def dot(a, b, dims=NN):
    return lax.dot_general(a, b, dims, preferred_element_type=f32)


def split(x):
    high = x.astype(bf16)
    return high, (x - high.astype(f32)).astype(bf16)


def stacked(x):
    return jnp.concatenate(split(x), axis=0)


def times(pair, high, low, dims=NN):
    both = dot(pair, high, dims)
    return both[:COLS] + both[COLS:] + dot(pair[:COLS], low, dims)


def times_wide(pair, both):
    out = dot(pair, both)
    out = out[:COLS] + out[COLS:]
    return out[:, :TILE] + out[:, TILE:]


def exact(a, b, dims):
    return lax.dot_general(
        a, b, dims, precision=lax.Precision.HIGHEST, preferred_element_type=f32
    )


def kernel(
    gx, gy,
    cols_h, rows_h, bounds_h, diag_h, start_h, tiles_h, faces_h,
    basis_h, proj,
    cols_s, rows_s, bounds_s, cols_v, rows_v, diag, stage, fstage,
    tn_h0, tn_l0, tt_h0, tt_l0, tn_h1, tn_l1, tt_h1, tt_l1, cn, ct,
    vb, vs, acc, scat, terms, low, down_s, down_r, up_s, hot, ys, fys,
    pad, gbuf0, gbuf1, sbuf0, sbuf1,
    stage_sem, fstage_sem, start_sem, small_sem, out_sem,
    down_ss, down_rs, up_ss, up_rs, red_ss, red_rs,
):
    u, v = lax.axis_index("gx"), lax.axis_index("gy")
    held = (tn_h0, tn_l0, tt_h0, tt_l0), (tn_h1, tn_l1, tt_h1, tt_l1)
    nodes = float(gx * gy * ROWS * TILE)

    def stage_copy(group):
        slot = lax.rem(group, SLOTS)
        return pltpu.make_async_copy(
            tiles_h.at[pl.ds(group * GROUP, GROUP)], stage.at[slot], stage_sem.at[slot]
        )

    pairs = (
        (cols_h, cols_v), (rows_h, rows_v), (rows_h, rows_s), (cols_h, cols_s),
        (bounds_h, bounds_s), (diag_h, diag),
    )
    small = [pltpu.make_async_copy(a, b, small_sem.at[n]) for n, (a, b) in enumerate(pairs)]
    for copy in small[:2]:
        copy.start()
    start_copy = pltpu.make_async_copy(start_h, vb.at[0], start_sem)
    start_copy.start()
    for copy in small[2:]:
        copy.start()
    face_copies = [
        pltpu.make_async_copy(
            faces_h.at[pl.ds(axis * FROWS, FROWS)],
            fstage.at[pl.ds(axis * FROWS, FROWS)],
            fstage_sem.at[axis],
        )
        for axis in range(2)
    ]
    face_copies[1].start()
    face_copies[0].start()

    def past(me, step, size):
        other = me + step
        return jnp.where(other >= size, other - size, other)

    sums = (
        (gx, u, [(past(u, step, gx), v) for step in range(1, gx)]),
        (gy, v, [(u, past(v, step, gy)) for step in range(1, gy)]),
    )
    lower = sums[0][2][gx - 2], sums[1][2][gy - 2]
    upper = sums[0][2][0], sums[1][2][0]
    barrier = pltpu.get_barrier_semaphore()
    greeted = sums[0][2] + sums[1][2]
    for peer in greeted:
        pl.semaphore_signal(barrier, inc=1, device_id=peer, device_id_type=MESH)

    def down_copy(axis, slot):
        return pltpu.make_async_remote_copy(
            src_ref=down_s.at[slot, axis], dst_ref=down_r.at[slot, axis],
            send_sem=down_ss.at[slot, axis], recv_sem=down_rs.at[slot, axis],
            device_id=lower[axis], device_id_type=MESH,
        )

    def up_copy(axis, slot):
        return pltpu.make_async_remote_copy(
            src_ref=up_s.at[slot, axis], dst_ref=low.at[slot, axis],
            send_sem=up_ss.at[slot, axis], recv_sem=up_rs.at[slot, axis],
            device_id=upper[axis], device_id_type=MESH,
        )

    tall = lax.broadcasted_iota(jnp.int32, (ROWS, FROWS), 0)
    taller = lax.broadcasted_iota(jnp.int32, (ROWS, ROWS), 0)
    for copy in small:
        copy.wait()
    for k in range(NB):
        match = (cols_v[k : k + 1, :] == taller).astype(f32)
        hot[:, k * ROWS : (k + 1) * ROWS] = match
    hot[:, LOCAL:] = jnp.zeros((ROWS, 128), f32)
    has_upper = ((u < gx - 1).astype(f32), (v < gy - 1).astype(f32))
    has_lower = ((u > 0).astype(f32), (v > 0).astype(f32))
    for axis in range(2):
        gain = (rows_v[2 * axis : 2 * axis + 1, :] == tall).astype(f32) * has_upper[axis]
        hot[:, LOCAL + axis * FROWS : LOCAL + (axis + 1) * FROWS] = gain
        lost = (rows_v[2 * axis + 1 : 2 * axis + 2, :] == tall).astype(f32) * has_lower[axis]
        hot[:, TERMS + axis * FROWS : TERMS + (axis + 1) * FROWS] = lost
    terms[(LOCAL + 2 * FROWS) * COLS :, :] = jnp.zeros(
        ((TERMS - LOCAL - 2 * FROWS) * COLS, TILE), f32
    )
    pad[...] = jnp.zeros((COLS, 128), f32)

    low_end = jnp.full((COLS, TILE), bounds_s[0], f32)
    high_end = jnp.full((COLS, TILE), bounds_s[1], f32)
    inverse_half = 2.0 / (high_end - low_end)
    centre = (high_end + low_end) * 0.5

    start_copy.wait()

    def split_rows(i, _):
        vs[i] = stacked(vb[0, i])
        return 0

    lax.fori_loop(0, ROWS, split_rows, 0, unroll=8)

    def fill_down(k, slot):
        def one(j, _):
            for axis in range(2):
                down_s[slot, axis, j] = vb[k, rows_s[2 * axis + 1, j]]
            return 0

        lax.fori_loop(0, FROWS, one, 0, unroll=8)

    def products(slot, axis, first):
        def one(j, _):
            f = axis * FROWS + j
            if first:
                high, small = split(fstage[f])
                both = jnp.concatenate([high, small], axis=1)
                cn[f] = both
                ct[f, :, :TILE] = jnp.transpose(high)
                ct[f, :, TILE:] = jnp.transpose(small)
            else:
                both = cn[f]
            up_s[slot, axis, j] = times_wide(vs[rows_s[2 * axis, j]], both)
            return 0

        lax.fori_loop(0, FROWS, one, 0, unroll=True)

    def gather4(i):
        return jnp.concatenate([vs[cols_s[k, i]] for k in range(NB)], axis=1)

    def convert_row(part, t, slot, r):
        tn_h, tn_l, tt_h, tt_l = held[part]
        for k in range(NB):
            high, small = split(stage[slot, r, k])
            lanes = slice(k * TILE, (k + 1) * TILE)
            tn_h[t, :, lanes] = high
            tn_l[t, :, lanes] = small
            tt_h[t, lanes, :] = jnp.transpose(high)
            tt_l[t, lanes, :] = jnp.transpose(small)

    def full_row(part, t, i):
        tn_h, tn_l, tt_h, tt_l = held[part]
        acc[i] = times(gather4(i), tt_h[t], tt_l[t])
        back = times(vs[i], tn_h[t], tn_l[t])
        for k in range(NB):
            at = pl.multiple_of((k * ROWS + i) * COLS, COLS)
            terms[pl.ds(at, COLS), :] = back[:, k * TILE : (k + 1) * TILE]

    def gains(slot):
        def one(j, _):
            for axis in range(2):
                f = axis * FROWS + j
                at = pl.multiple_of((LOCAL + f) * COLS, COLS)
                terms[pl.ds(at, COLS), :] = times_wide(
                    stacked(down_r[slot, axis, j]), ct[f]
                )
            return 0

        lax.fori_loop(0, FROWS, one, 0, unroll=True)

    def scatter(slot):
        places = hot[...].astype(bf16)
        got = low.at[slot].reshape(2 * FROWS * COLS, TILE)
        for c in range(COLS):
            column = jnp.concatenate(
                [
                    terms[pl.ds(c, TERMS, stride=COLS), :],
                    got[pl.ds(c, 2 * FROWS, stride=COLS), :],
                ],
                axis=0,
            )
            out = dot(places, jnp.concatenate(split(column), axis=1))
            scat[pl.ds(c, ROWS, stride=COLS), :] = out[:, :TILE] + out[:, TILE:]

    def update(k, before, scale, keep):
        def one(i, _):
            block = vb[k, i]
            at = pl.multiple_of(i * COLS, COLS)
            applied = diag[pl.ds(i, 1), :] * block + acc[i] + scat[pl.ds(at, COLS), :]
            new = scale * (applied - centre * block)
            if keep:
                new = new - vb[before, i]
            vb[k + 1, i] = new
            vs[i] = stacked(new)
            return 0

        lax.fori_loop(0, ROWS, one, 0, unroll=8)

    def apply(k, first):
        slot = lax.rem(k, 2)
        fill_down(k, slot)
        if first:
            pl.semaphore_wait(barrier, len(greeted))
        down_copy(1, slot).start()
        down_copy(0, slot).start()
        for axis in (1, 0):
            if first:
                face_copies[axis].wait()
                if axis == 1:
                    for group in range(SLOTS):
                        stage_copy(group).start()
            products(slot, axis, first)
            up_copy(axis, slot).start()

        def convert_group(part, pair, r):
            convert_row(part, pair * GROUP + r, lax.rem(2 * pair + part, SLOTS), r)

        def full_group(part, pair, r):
            full_row(part, pair * GROUP + r, (2 * pair + part) * GROUP + r)

        if first:
            stage_copy(0).wait()
            for r in range(GROUP):
                convert_group(0, 0, r)

            def two_groups(pair, _):
                @pl.when(pair < NGROUPS // 2 - 2)
                def _():
                    stage_copy(2 * pair + 4).start()

                stage_copy(2 * pair + 1).wait()
                for r in range(GROUP):
                    convert_group(1, pair, r)
                    full_group(0, pair, r)

                @pl.when(pair < NGROUPS // 2 - 2)
                def _():
                    stage_copy(2 * pair + 5).start()

                stage_copy(2 * pair + 2).wait()
                for r in range(GROUP):
                    convert_group(0, pair + 1, r)
                    full_group(1, pair, r)
                return 0

            lax.fori_loop(0, NGROUPS // 2 - 1, two_groups, 0)
            last = NGROUPS // 2 - 1
            stage_copy(NGROUPS - 1).wait()
            for r in range(GROUP):
                convert_group(1, last, r)
                full_group(0, last, r)
            for r in range(GROUP):
                full_group(1, last, r)
        else:

            def plain(two, _):
                for pair in (2 * two, 2 * two + 1):
                    for part in range(2):
                        for r in range(GROUP):
                            full_group(part, pair, r)
                return 0

            lax.fori_loop(0, NGROUPS // 4, plain, 0)
        for axis in range(2):
            down_copy(axis, slot).wait()
        gains(slot)
        for axis in range(2):
            up_copy(axis, slot).wait()
        scatter(slot)

    apply(0, True)
    update(0, 0, inverse_half, False)

    def later(k, _):
        apply(k, False)
        update(k, k - 1, 2.0 * inverse_half, True)
        return 0

    lax.fori_loop(1, 3, later, 0)

    def pack(x):
        pad[:, 0 : 2 * COLS] = x[:COLS] + x[COLS:]
        full = pad[...]
        full = jnp.where(at < COLS, full + pltpu.roll(full, 128 - COLS, 1), 0.0)
        return full[:8] + pltpu.roll(full[8:], 64, 1)

    lanes = lax.broadcasted_iota(jnp.int32, (8, 128), 1)
    at = lax.broadcasted_iota(jnp.int32, (COLS, 128), 1)

    def unpack(p):
        top = jnp.where(lanes < COLS, p, 0.0)
        bottom = jnp.where(lanes < COLS, pltpu.roll(p, 64, 1), 0.0)
        return jnp.concatenate([top, bottom], axis=0)

    buffers = (gbuf0, gbuf1), (sbuf0, sbuf1)

    def reduce_copies(which, stage_no):
        _, me, peers = sums[stage_no]
        own = buffers[which][stage_no].at[me]
        base = (which * 2 + stage_no) * gy
        return [
            pltpu.make_async_remote_copy(
                src_ref=own, dst_ref=own,
                send_sem=red_ss.at[base + n], recv_sem=red_rs.at[base + n],
                device_id=peer, device_id_type=MESH,
            )
            for n, peer in enumerate(peers)
        ]

    def reduce_start(which, stage_no, value):
        buffers[which][stage_no][sums[stage_no][1]] = value
        copies = reduce_copies(which, stage_no)
        far = [(abs((n + 1) % 4 - 2) + abs((n + 1) // 4 - 2), n) for n in range(len(copies))]
        for _, n in sorted(far):
            copies[n].start()

    def reduce_end(which, stage_no):
        size = sums[stage_no][0]
        copies = reduce_copies(which, stage_no)
        for copy in copies:
            copy.wait_send()
        for copy in copies:
            copy.wait_recv()
        parts = [buffers[which][stage_no][source] for source in range(size)]
        while len(parts) > 1:
            parts = [a + b for a, b in zip(parts[0::2], parts[1::2])]
        return parts[0]

    def inner(count, left, right):
        total = jnp.zeros((2 * COLS, 2 * COLS), f32)
        for g in range(count // BIG):
            a = jnp.concatenate([left(g * BIG + r) for r in range(BIG)], axis=1)
            b = jnp.concatenate([right(g * BIG + r) for r in range(BIG)], axis=1)
            total = total + dot(a, b, NT)
        return total

    fill_down(3, 1)
    down_copy(1, 1).start()
    down_copy(0, 1).start()
    gram = inner(ROWS, lambda i: vs[i], lambda i: vs[i])
    reduce_start(0, 0, pack(gram))

    def half_groups(pair, _):
        for part in range(2):
            high, small = held[part][2:]
            for r in range(GROUP):
                i = (2 * pair + part) * GROUP + r
                t = pair * GROUP + r
                image = times(gather4(i), high[t], small[t])
                image = image + 0.5 * (diag[pl.ds(i, 1), :] * vb[3, i])
                ys[i] = stacked(image)
        return 0

    lax.fori_loop(0, NGROUPS // 4, lambda two, c: half_groups(2 * two + 1, half_groups(2 * two, c)), 0)
    reduce_start(0, 1, reduce_end(0, 0))
    half = inner(ROWS, lambda i: vs[i], lambda i: ys[i])
    for axis in range(2):
        down_copy(axis, 1).wait()

    def half_face(j, _):
        for axis in range(2):
            f = axis * FROWS + j
            image = times_wide(stacked(down_r[1, axis, j]), ct[f])
            fys[f] = stacked(image * has_upper[axis])
        return 0

    lax.fori_loop(0, FROWS, half_face, 0, unroll=True)
    half = half + inner(
        2 * FROWS, lambda f: vs[rows_s[2 * (f // FROWS), f % FROWS]], lambda f: fys[f]
    )
    reduce_start(1, 0, pack(half))
    reduce_start(1, 1, reduce_end(1, 0))

    work = unpack(reduce_end(0, 1)) * (1.0 / nodes)
    down = lax.broadcasted_iota(jnp.int32, (COLS, 128), 0)
    work = work + (at == down + 64).astype(f32)
    for j in range(COLS):
        pivot = work[j : j + 1, :]
        root = 1.0 / jnp.sqrt(pivot[:, j : j + 1])
        pivot = pivot * root
        factor = work[:, j : j + 1] * root
        work = jnp.where(down > j, work - factor * pivot, jnp.where(down == j, pivot, work))
    inverse = jnp.where(at < COLS, pltpu.roll(work, 64, 1), 0.0)
    high, small = split(inverse)
    twice = high.astype(f32)
    twice = twice + pltpu.roll(twice, COLS, 1)
    mixer = jnp.concatenate([twice.astype(bf16), small], axis=0)[:, : 2 * COLS]


    for g in range(ROWS // 4):
        four = jnp.concatenate([vs[g * 4 + r] for r in range(4)], axis=1)
        out = dot(mixer, four)
        out = out[:COLS] + out[COLS:]
        for r in range(4):
            vb[0, g * 4 + r] = out[:, r * TILE : (r + 1) * TILE]
    out_copy = pltpu.make_async_copy(vb.at[0], basis_h, out_sem)
    out_copy.start()

    summed = unpack(reduce_end(1, 1))[:, :COLS] * (1.0 / nodes)
    narrow = inverse[:, :COLS]
    both = exact(narrow, summed, NN) + exact(narrow, summed, NT)
    proj[...] = exact(both, narrow, NT)
    out_copy.wait()


def hand_over(basis_in, proj_in, basis, proj, held, small, sems):
    parts = ROWS // GROUP
    ins = [
        pltpu.make_async_copy(
            basis_in.at[pl.ds(g * GROUP, GROUP)], held.at[pl.ds(g * GROUP, GROUP)], sems.at[0, g]
        )
        for g in range(parts)
    ] + [pltpu.make_async_copy(proj_in, small, sems.at[0, parts])]
    outs = [
        pltpu.make_async_copy(
            held.at[pl.ds(g * GROUP, GROUP)], basis.at[pl.ds(g * GROUP, GROUP)], sems.at[1, g]
        )
        for g in range(parts)
    ] + [pltpu.make_async_copy(small, proj, sems.at[1, parts])]
    for copy in ins:
        copy.start()
    for first, second in zip(ins, outs):
        first.wait()
        second.start()
    for copy in outs:
        copy.wait()


def run(gx, gy, cols, rows, bounds, diag, start, tiles, faces):
    hbm = pl.BlockSpec(memory_space=pl.ANY)
    vmem = pl.BlockSpec(memory_space=pltpu.VMEM)
    faces_n = 2 * FROWS
    shapes = (
        jax.ShapeDtypeStruct((ROWS, COLS, TILE), f32),
        jax.ShapeDtypeStruct((COLS, COLS), f32),
    )
    results = pl.pallas_call(
        functools.partial(kernel, gx, gy),
        out_shape=shapes,
        in_specs=[hbm] * 7,
        out_specs=(hbm, vmem),
        scratch_shapes=[
            pltpu.SMEM((NB, ROWS), jnp.int32),
            pltpu.SMEM((4, FROWS), jnp.int32),
            pltpu.SMEM((2,), f32),
            pltpu.VMEM((NB, ROWS), jnp.int32),
            pltpu.VMEM((4, FROWS), jnp.int32),
            pltpu.VMEM((ROWS, TILE), f32),
            pltpu.VMEM((SLOTS, GROUP, NB, TILE, TILE), f32),
            pltpu.VMEM((faces_n, TILE, TILE), f32),
            *(
                [pltpu.VMEM((ROWS // 2, TILE, NB * TILE), bf16)] * 2
                + [pltpu.VMEM((ROWS // 2, NB * TILE, TILE), bf16)] * 2
            )
            * 2,
            pltpu.VMEM((faces_n, TILE, 2 * TILE), bf16),
            pltpu.VMEM((faces_n, TILE, 2 * TILE), bf16),
            pltpu.VMEM((4, ROWS, COLS, TILE), f32),
            pltpu.VMEM((ROWS, 2 * COLS, TILE), bf16),
            pltpu.VMEM((ROWS, COLS, TILE), f32),
            pltpu.VMEM((ROWS * COLS, TILE), f32),
            pltpu.VMEM((TERMS * COLS, TILE), f32),
            pltpu.VMEM((2, 2, FROWS, COLS, TILE), f32),
            pltpu.VMEM((2, 2, FROWS, COLS, TILE), f32),
            pltpu.VMEM((2, 2, FROWS, COLS, TILE), f32),
            pltpu.VMEM((2, 2, FROWS, COLS, TILE), f32),
            pltpu.VMEM((ROWS, 384), f32),
            pltpu.VMEM((ROWS, 2 * COLS, TILE), bf16),
            pltpu.VMEM((faces_n, 2 * COLS, TILE), bf16),
            pltpu.VMEM((COLS, 128), f32),
            *(
                pltpu.VMEM((gx, 8, 128), f32),
                pltpu.VMEM((gy, 8, 128), f32),
            )
            * 2,
            pltpu.SemaphoreType.DMA((SLOTS,)),
            pltpu.SemaphoreType.DMA((2,)),
            pltpu.SemaphoreType.DMA,
            pltpu.SemaphoreType.DMA((6,)),
            pltpu.SemaphoreType.DMA,
            pltpu.SemaphoreType.DMA((2, 2)),
            pltpu.SemaphoreType.DMA((2, 2)),
            pltpu.SemaphoreType.DMA((2, 2)),
            pltpu.SemaphoreType.DMA((2, 2)),
            pltpu.SemaphoreType.DMA((4 * gy,)),
            pltpu.SemaphoreType.DMA((4 * gy,)),
        ],
        compiler_params=pltpu.CompilerParams(
            collective_id=0, has_side_effects=True, vmem_limit_bytes=62 << 20
        ),
    )(cols, rows, bounds, diag, start, tiles, faces)
    return pl.pallas_call(
        hand_over,
        out_shape=shapes,
        in_specs=[hbm] * 2,
        out_specs=(hbm, hbm),
        scratch_shapes=[
            pltpu.VMEM((ROWS, COLS, TILE), f32),
            pltpu.VMEM((COLS, COLS), f32),
            pltpu.SemaphoreType.DMA((2, ROWS // GROUP + 1)),
        ],
    )(*results)


def shards(start_block, tiles, tile_cols, node_diag, face_tiles, face_rows, filter_bounds):
    gx, gy = lax.axis_size("gx"), lax.axis_size("gy")
    basis, projected = run(
        gx, gy,
        tile_cols[0, 0].T, face_rows[0, 0], filter_bounds, node_diag[0, 0], start_block[0, 0],
        tiles[0, 0], face_tiles[0, 0].reshape(2 * FROWS, TILE, TILE),
    )
    return basis[None, None], projected


def solution(mesh):
    in_specs = (
        P("gx", "gy", None, None, None),
        P("gx", "gy", None, None, None, None),
        P("gx", "gy", None, None),
        P("gx", "gy", None, None),
        P("gx", "gy", None, None, None, None),
        P("gx", "gy", None, None),
        P(),
    )
    out_specs = (P("gx", "gy", None, None, None), P())
    return jax.shard_map(shards, mesh=mesh, in_specs=in_specs, out_specs=out_specs, check_vma=False)
```

```python
import functools

import jax
import jax.numpy as jnp
from jax import lax
from jax.experimental import pallas as pl
from jax.experimental.pallas import tpu as pltpu
from jax.sharding import PartitionSpec as P

MESH = pl.DeviceIdType.MESH
f32, bf16 = jnp.float32, jnp.bfloat16
NN = (((1,), (0,)), ((), ()))
NT = (((1,), (1,)), ((), ()))
ROWS, NB, COLS, TILE, FROWS = 64, 4, 16, 128, 24
GROUP = 8
NGROUPS = ROWS // GROUP
LOCAL = ROWS * NB
SLOTS = 4
BIG = 16
TERMS = 336


def dot(a, b, dims=NN):
    return lax.dot_general(a, b, dims, preferred_element_type=f32)


def split(x):
    high = x.astype(bf16)
    return high, (x - high.astype(f32)).astype(bf16)


def stacked(x):
    return jnp.concatenate(split(x), axis=0)


def times(pair, high, low, dims=NN):
    both = dot(pair, high, dims)
    return both[:COLS] + both[COLS:] + dot(pair[:COLS], low, dims)


def times_wide(pair, both):
    out = dot(pair, both)
    out = out[:COLS] + out[COLS:]
    return out[:, :TILE] + out[:, TILE:]


def exact(a, b, dims):
    return lax.dot_general(
        a, b, dims, precision=lax.Precision.HIGHEST, preferred_element_type=f32
    )


def kernel(
    gx, gy,
    cols_h, rows_h, bounds_h, diag_h, start_h, tiles_h, faces_h,
    basis_h, proj,
    cols_s, rows_s, bounds_s, cols_v, rows_v, diag, stage, fstage,
    tn_h0, tn_l0, tt_h0, tt_l0, tn_h1, tn_l1, tt_h1, tt_l1, cn, ct,
    vb, vs, acc, scat, terms, low, down_s, down_r, up_s, hot, places, ys, fys,
    pad, gbuf0, gbuf1, sbuf0, sbuf1,
    stage_sem, fstage_sem, start_sem, small_sem, out_sem,
    down_ss, down_rs, up_ss, up_rs, red_ss, red_rs,
):
    u, v = lax.axis_index("gx"), lax.axis_index("gy")
    held = (tn_h0, tn_l0, tt_h0, tt_l0), (tn_h1, tn_l1, tt_h1, tt_l1)
    nodes = float(gx * gy * ROWS * TILE)

    def stage_copy(group):
        slot = lax.rem(group, SLOTS)
        return pltpu.make_async_copy(
            tiles_h.at[pl.ds(group * GROUP, GROUP)], stage.at[slot], stage_sem.at[slot]
        )

    pairs = (
        (cols_h, cols_v), (rows_h, rows_v), (rows_h, rows_s), (cols_h, cols_s),
        (bounds_h, bounds_s), (diag_h, diag),
    )
    small = [pltpu.make_async_copy(a, b, small_sem.at[n]) for n, (a, b) in enumerate(pairs)]
    for copy in small[:2]:
        copy.start()
    start_copy = pltpu.make_async_copy(start_h, vb.at[0], start_sem)
    start_copy.start()
    for copy in small[2:]:
        copy.start()
    face_copies = [
        pltpu.make_async_copy(
            faces_h.at[pl.ds(axis * FROWS, FROWS)],
            fstage.at[pl.ds(axis * FROWS, FROWS)],
            fstage_sem.at[axis],
        )
        for axis in range(2)
    ]
    face_copies[1].start()
    face_copies[0].start()

    def past(me, step, size):
        other = me + step
        return jnp.where(other >= size, other - size, other)

    sums = (
        (gx, u, [(past(u, step, gx), v) for step in range(1, gx)]),
        (gy, v, [(u, past(v, step, gy)) for step in range(1, gy)]),
    )
    lower = sums[0][2][gx - 2], sums[1][2][gy - 2]
    upper = sums[0][2][0], sums[1][2][0]
    barrier = pltpu.get_barrier_semaphore()
    greeted = sums[0][2] + sums[1][2]
    for peer in greeted:
        pl.semaphore_signal(barrier, inc=1, device_id=peer, device_id_type=MESH)

    def down_copy(axis, slot):
        return pltpu.make_async_remote_copy(
            src_ref=down_s.at[slot, axis], dst_ref=down_r.at[slot, axis],
            send_sem=down_ss.at[slot, axis], recv_sem=down_rs.at[slot, axis],
            device_id=lower[axis], device_id_type=MESH,
        )

    def up_copy(axis, slot):
        return pltpu.make_async_remote_copy(
            src_ref=up_s.at[slot, axis], dst_ref=low.at[slot, axis],
            send_sem=up_ss.at[slot, axis], recv_sem=up_rs.at[slot, axis],
            device_id=upper[axis], device_id_type=MESH,
        )

    tall = lax.broadcasted_iota(jnp.int32, (ROWS, FROWS), 0)
    taller = lax.broadcasted_iota(jnp.int32, (ROWS, ROWS), 0)
    for copy in small:
        copy.wait()
    for k in range(NB):
        match = (cols_v[k : k + 1, :] == taller).astype(f32)
        hot[:, k * ROWS : (k + 1) * ROWS] = match
    hot[:, LOCAL:] = jnp.zeros((ROWS, 128), f32)
    has_upper = ((u < gx - 1).astype(f32), (v < gy - 1).astype(f32))
    has_lower = ((u > 0).astype(f32), (v > 0).astype(f32))
    for axis in range(2):
        gain = (rows_v[2 * axis : 2 * axis + 1, :] == tall).astype(f32) * has_upper[axis]
        hot[:, LOCAL + axis * FROWS : LOCAL + (axis + 1) * FROWS] = gain
        lost = (rows_v[2 * axis + 1 : 2 * axis + 2, :] == tall).astype(f32) * has_lower[axis]
        hot[:, TERMS + axis * FROWS : TERMS + (axis + 1) * FROWS] = lost
    places[...] = hot[...].astype(bf16)
    terms[(LOCAL + 2 * FROWS) * COLS :, :] = jnp.zeros(
        ((TERMS - LOCAL - 2 * FROWS) * COLS, TILE), f32
    )
    pad[...] = jnp.zeros((COLS, 128), f32)

    low_end = jnp.full((COLS, TILE), bounds_s[0], f32)
    high_end = jnp.full((COLS, TILE), bounds_s[1], f32)
    inverse_half = 2.0 / (high_end - low_end)
    centre = (high_end + low_end) * 0.5

    start_copy.wait()

    def split_rows(i, _):
        vs[i] = stacked(vb[0, i])
        return 0

    lax.fori_loop(0, ROWS, split_rows, 0, unroll=8)

    def fill_down(k, slot):
        def one(j, _):
            for axis in range(2):
                down_s[slot, axis, j] = vb[k, rows_s[2 * axis + 1, j]]
            return 0

        lax.fori_loop(0, FROWS, one, 0, unroll=8)

    def products(slot, axis, first):
        def one(j, _):
            f = axis * FROWS + j
            if first:
                high, small = split(fstage[f])
                both = jnp.concatenate([high, small], axis=1)
                cn[f] = both
                ct[f, :, :TILE] = jnp.transpose(high)
                ct[f, :, TILE:] = jnp.transpose(small)
            else:
                both = cn[f]
            up_s[slot, axis, j] = times_wide(vs[rows_s[2 * axis, j]], both)
            return 0

        lax.fori_loop(0, FROWS, one, 0, unroll=True)

    def gather4(i):
        return jnp.concatenate([vs[cols_s[k, i]] for k in range(NB)], axis=1)

    def convert_row(part, t, slot, r):
        tn_h, tn_l, tt_h, tt_l = held[part]
        for k in range(NB):
            high, small = split(stage[slot, r, k])
            lanes = slice(k * TILE, (k + 1) * TILE)
            tn_h[t, :, lanes] = high
            tn_l[t, :, lanes] = small
            tt_h[t, lanes, :] = jnp.transpose(high)
            tt_l[t, lanes, :] = jnp.transpose(small)

    def full_row(part, t, i):
        tn_h, tn_l, tt_h, tt_l = held[part]
        acc[i] = times(gather4(i), tt_h[t], tt_l[t])
        back = times(vs[i], tn_h[t], tn_l[t])
        for k in range(NB):
            at = pl.multiple_of((k * ROWS + i) * COLS, COLS)
            terms[pl.ds(at, COLS), :] = back[:, k * TILE : (k + 1) * TILE]

    def gains(slot):
        def one(j, _):
            for axis in range(2):
                f = axis * FROWS + j
                at = pl.multiple_of((LOCAL + f) * COLS, COLS)
                terms[pl.ds(at, COLS), :] = times_wide(
                    stacked(down_r[slot, axis, j]), ct[f]
                )
            return 0

        lax.fori_loop(0, FROWS, one, 0, unroll=True)

    def scatter(slot):
        got = low.at[slot].reshape(2 * FROWS * COLS, TILE)
        for c in range(COLS):
            column = jnp.concatenate(
                [
                    terms[pl.ds(c, TERMS, stride=COLS), :],
                    got[pl.ds(c, 2 * FROWS, stride=COLS), :],
                ],
                axis=0,
            )
            out = dot(places[...], jnp.concatenate(split(column), axis=1))
            scat[pl.ds(c, ROWS, stride=COLS), :] = out[:, :TILE] + out[:, TILE:]

    def update(k, before, scale, keep):
        def one(i, _):
            block = vb[k, i]
            at = pl.multiple_of(i * COLS, COLS)
            applied = diag[pl.ds(i, 1), :] * block + acc[i] + scat[pl.ds(at, COLS), :]
            new = scale * (applied - centre * block)
            if keep:
                new = new - vb[before, i]
            vb[k + 1, i] = new
            vs[i] = stacked(new)
            return 0

        lax.fori_loop(0, ROWS, one, 0, unroll=BIG)

    def apply(k, first):
        slot = lax.rem(k, 2)
        fill_down(k, slot)
        if first:
            pl.semaphore_wait(barrier, len(greeted))
        down_copy(1, slot).start()
        down_copy(0, slot).start()
        for axis in (1, 0):
            if first:
                face_copies[axis].wait()
                if axis == 1:
                    for group in range(SLOTS):
                        stage_copy(group).start()
            products(slot, axis, first)
            up_copy(axis, slot).start()

        def convert_group(part, pair, r):
            convert_row(part, pair * GROUP + r, lax.rem(2 * pair + part, SLOTS), r)

        def full_group(part, pair, r):
            full_row(part, pair * GROUP + r, (2 * pair + part) * GROUP + r)

        if first:
            stage_copy(0).wait()
            for r in range(GROUP):
                convert_group(0, 0, r)

            def two_groups(pair, _):
                @pl.when(pair < NGROUPS // 2 - 2)
                def _():
                    stage_copy(2 * pair + 4).start()

                stage_copy(2 * pair + 1).wait()
                for r in range(GROUP):
                    convert_group(1, pair, r)
                    full_group(0, pair, r)

                @pl.when(pair < NGROUPS // 2 - 2)
                def _():
                    stage_copy(2 * pair + 5).start()

                stage_copy(2 * pair + 2).wait()
                for r in range(GROUP):
                    convert_group(0, pair + 1, r)
                    full_group(1, pair, r)
                return 0

            lax.fori_loop(0, NGROUPS // 2 - 1, two_groups, 0)
            last = NGROUPS // 2 - 1
            stage_copy(NGROUPS - 1).wait()
            for r in range(GROUP):
                convert_group(1, last, r)
                full_group(0, last, r)
            for r in range(GROUP):
                full_group(1, last, r)
        else:

            def plain(two, _):
                for pair in (2 * two, 2 * two + 1):
                    for part in range(2):
                        for r in range(GROUP):
                            full_group(part, pair, r)
                return 0

            lax.fori_loop(0, NGROUPS // 4, plain, 0)
        for axis in range(2):
            down_copy(axis, slot).wait()
        gains(slot)
        for axis in range(2):
            up_copy(axis, slot).wait()
        scatter(slot)

    apply(0, True)
    update(0, 0, inverse_half, False)

    def later(k, _):
        apply(k, False)
        update(k, k - 1, 2.0 * inverse_half, True)
        return 0

    lax.fori_loop(1, 3, later, 0)

    def pack(x):
        pad[:, 0 : 2 * COLS] = x[:COLS] + x[COLS:]
        full = pad[...]
        full = jnp.where(at < COLS, full + pltpu.roll(full, 128 - COLS, 1), 0.0)
        return full[:8] + pltpu.roll(full[8:], 64, 1)

    lanes = lax.broadcasted_iota(jnp.int32, (8, 128), 1)
    at = lax.broadcasted_iota(jnp.int32, (COLS, 128), 1)

    def unpack(p):
        top = jnp.where(lanes < COLS, p, 0.0)
        bottom = jnp.where(lanes < COLS, pltpu.roll(p, 64, 1), 0.0)
        return jnp.concatenate([top, bottom], axis=0)

    buffers = (gbuf0, gbuf1), (sbuf0, sbuf1)

    def reduce_copies(which, stage_no):
        _, me, peers = sums[stage_no]
        own = buffers[which][stage_no].at[me]
        base = (which * 2 + stage_no) * gy
        return [
            pltpu.make_async_remote_copy(
                src_ref=own, dst_ref=own,
                send_sem=red_ss.at[base + n], recv_sem=red_rs.at[base + n],
                device_id=peer, device_id_type=MESH,
            )
            for n, peer in enumerate(peers)
        ]

    def reduce_start(which, stage_no, value):
        buffers[which][stage_no][sums[stage_no][1]] = value
        copies = reduce_copies(which, stage_no)
        far = [(abs((n + 1) % 4 - 2) + abs((n + 1) // 4 - 2), n) for n in range(len(copies))]
        for _, n in sorted(far):
            copies[n].start()

    def reduce_end(which, stage_no):
        size = sums[stage_no][0]
        copies = reduce_copies(which, stage_no)
        for copy in copies:
            copy.wait_send()
        for copy in copies:
            copy.wait_recv()
        parts = [buffers[which][stage_no][source] for source in range(size)]
        while len(parts) > 1:
            parts = [a + b for a, b in zip(parts[0::2], parts[1::2])]
        return parts[0]

    def inner(count, left, right):
        total = jnp.zeros((2 * COLS, 2 * COLS), f32)
        for g in range(count // BIG):
            a = jnp.concatenate([left(g * BIG + r) for r in range(BIG)], axis=1)
            b = jnp.concatenate([right(g * BIG + r) for r in range(BIG)], axis=1)
            total = total + dot(a, b, NT)
        return total

    fill_down(3, 1)
    down_copy(1, 1).start()
    down_copy(0, 1).start()
    gram = inner(ROWS, lambda i: vs[i], lambda i: vs[i])
    reduce_start(0, 0, pack(gram))

    def half_groups(pair, _):
        for part in range(2):
            high, small = held[part][2:]
            for r in range(GROUP):
                i = (2 * pair + part) * GROUP + r
                t = pair * GROUP + r
                image = times(gather4(i), high[t], small[t])
                image = image + 0.5 * (diag[pl.ds(i, 1), :] * vb[3, i])
                ys[i] = stacked(image)
        return 0

    lax.fori_loop(0, NGROUPS // 4, lambda two, c: half_groups(2 * two + 1, half_groups(2 * two, c)), 0)
    reduce_start(0, 1, reduce_end(0, 0))
    half = inner(ROWS, lambda i: vs[i], lambda i: ys[i])
    for axis in range(2):
        down_copy(axis, 1).wait()

    def half_face(j, _):
        for axis in range(2):
            f = axis * FROWS + j
            image = times_wide(stacked(down_r[1, axis, j]), ct[f])
            fys[f] = stacked(image * has_upper[axis])
        return 0

    lax.fori_loop(0, FROWS, half_face, 0, unroll=True)
    half = half + inner(
        2 * FROWS, lambda f: vs[rows_s[2 * (f // FROWS), f % FROWS]], lambda f: fys[f]
    )
    reduce_start(1, 0, pack(half))
    reduce_start(1, 1, reduce_end(1, 0))

    work = unpack(reduce_end(0, 1)) * (1.0 / nodes)
    down = lax.broadcasted_iota(jnp.int32, (COLS, 128), 0)
    work = work + (at == down + 64).astype(f32)
    for j in range(COLS):
        pivot = work[j : j + 1, :]
        root = 1.0 / jnp.sqrt(pivot[:, j : j + 1])
        pivot = pivot * root
        factor = work[:, j : j + 1] * root
        work = jnp.where(down > j, work - factor * pivot, jnp.where(down == j, pivot, work))
    inverse = jnp.where(at < COLS, pltpu.roll(work, 64, 1), 0.0)
    high, small = split(inverse)
    twice = high.astype(f32)
    twice = twice + pltpu.roll(twice, COLS, 1)
    mixer = jnp.concatenate([twice.astype(bf16), small], axis=0)[:, : 2 * COLS]


    for g in range(ROWS // 4):
        four = jnp.concatenate([vs[g * 4 + r] for r in range(4)], axis=1)
        out = dot(mixer, four)
        out = out[:COLS] + out[COLS:]
        for r in range(4):
            vb[0, g * 4 + r] = out[:, r * TILE : (r + 1) * TILE]
    out_copy = pltpu.make_async_copy(vb.at[0], basis_h, out_sem)
    out_copy.start()

    summed = unpack(reduce_end(1, 1))[:, :COLS] * (1.0 / nodes)
    narrow = inverse[:, :COLS]
    both = exact(narrow, summed, NN) + exact(narrow, summed, NT)
    proj[...] = exact(both, narrow, NT)
    out_copy.wait()


def hand_over(basis_in, proj_in, basis, proj, held, small, sems):
    parts = ROWS // GROUP
    ins = [
        pltpu.make_async_copy(
            basis_in.at[pl.ds(g * GROUP, GROUP)], held.at[pl.ds(g * GROUP, GROUP)], sems.at[0, g]
        )
        for g in range(parts)
    ] + [pltpu.make_async_copy(proj_in, small, sems.at[0, parts])]
    outs = [
        pltpu.make_async_copy(
            held.at[pl.ds(g * GROUP, GROUP)], basis.at[pl.ds(g * GROUP, GROUP)], sems.at[1, g]
        )
        for g in range(parts)
    ] + [pltpu.make_async_copy(small, proj, sems.at[1, parts])]
    for copy in ins:
        copy.start()
    for first, second in zip(ins, outs):
        first.wait()
        second.start()
    for copy in outs:
        copy.wait()


def run(gx, gy, cols, rows, bounds, diag, start, tiles, faces):
    hbm = pl.BlockSpec(memory_space=pl.ANY)
    vmem = pl.BlockSpec(memory_space=pltpu.VMEM)
    faces_n = 2 * FROWS
    shapes = (
        jax.ShapeDtypeStruct((ROWS, COLS, TILE), f32),
        jax.ShapeDtypeStruct((COLS, COLS), f32),
    )
    results = pl.pallas_call(
        functools.partial(kernel, gx, gy),
        out_shape=shapes,
        in_specs=[hbm] * 7,
        out_specs=(hbm, vmem),
        scratch_shapes=[
            pltpu.SMEM((NB, ROWS), jnp.int32),
            pltpu.SMEM((4, FROWS), jnp.int32),
            pltpu.SMEM((2,), f32),
            pltpu.VMEM((NB, ROWS), jnp.int32),
            pltpu.VMEM((4, FROWS), jnp.int32),
            pltpu.VMEM((ROWS, TILE), f32),
            pltpu.VMEM((SLOTS, GROUP, NB, TILE, TILE), f32),
            pltpu.VMEM((faces_n, TILE, TILE), f32),
            *(
                [pltpu.VMEM((ROWS // 2, TILE, NB * TILE), bf16)] * 2
                + [pltpu.VMEM((ROWS // 2, NB * TILE, TILE), bf16)] * 2
            )
            * 2,
            pltpu.VMEM((faces_n, TILE, 2 * TILE), bf16),
            pltpu.VMEM((faces_n, TILE, 2 * TILE), bf16),
            pltpu.VMEM((4, ROWS, COLS, TILE), f32),
            pltpu.VMEM((ROWS, 2 * COLS, TILE), bf16),
            pltpu.VMEM((ROWS, COLS, TILE), f32),
            pltpu.VMEM((ROWS * COLS, TILE), f32),
            pltpu.VMEM((TERMS * COLS, TILE), f32),
            pltpu.VMEM((2, 2, FROWS, COLS, TILE), f32),
            pltpu.VMEM((2, 2, FROWS, COLS, TILE), f32),
            pltpu.VMEM((2, 2, FROWS, COLS, TILE), f32),
            pltpu.VMEM((2, 2, FROWS, COLS, TILE), f32),
            pltpu.VMEM((ROWS, 384), f32),
            pltpu.VMEM((ROWS, 384), bf16),
            pltpu.VMEM((ROWS, 2 * COLS, TILE), bf16),
            pltpu.VMEM((faces_n, 2 * COLS, TILE), bf16),
            pltpu.VMEM((COLS, 128), f32),
            *(
                pltpu.VMEM((gx, 8, 128), f32),
                pltpu.VMEM((gy, 8, 128), f32),
            )
            * 2,
            pltpu.SemaphoreType.DMA((SLOTS,)),
            pltpu.SemaphoreType.DMA((2,)),
            pltpu.SemaphoreType.DMA,
            pltpu.SemaphoreType.DMA((6,)),
            pltpu.SemaphoreType.DMA,
            pltpu.SemaphoreType.DMA((2, 2)),
            pltpu.SemaphoreType.DMA((2, 2)),
            pltpu.SemaphoreType.DMA((2, 2)),
            pltpu.SemaphoreType.DMA((2, 2)),
            pltpu.SemaphoreType.DMA((4 * gy,)),
            pltpu.SemaphoreType.DMA((4 * gy,)),
        ],
        compiler_params=pltpu.CompilerParams(
            collective_id=0, has_side_effects=True, vmem_limit_bytes=62 << 20
        ),
    )(cols, rows, bounds, diag, start, tiles, faces)
    return pl.pallas_call(
        hand_over,
        out_shape=shapes,
        in_specs=[hbm] * 2,
        out_specs=(hbm, hbm),
        scratch_shapes=[
            pltpu.VMEM((ROWS, COLS, TILE), f32),
            pltpu.VMEM((COLS, COLS), f32),
            pltpu.SemaphoreType.DMA((2, ROWS // GROUP + 1)),
        ],
    )(*results)


def shards(start_block, tiles, tile_cols, node_diag, face_tiles, face_rows, filter_bounds):
    gx, gy = lax.axis_size("gx"), lax.axis_size("gy")
    basis, projected = run(
        gx, gy,
        tile_cols[0, 0].T, face_rows[0, 0], filter_bounds, node_diag[0, 0], start_block[0, 0],
        tiles[0, 0], face_tiles[0, 0].reshape(2 * FROWS, TILE, TILE),
    )
    return basis[None, None], projected


def solution(mesh):
    in_specs = (
        P("gx", "gy", None, None, None),
        P("gx", "gy", None, None, None, None),
        P("gx", "gy", None, None),
        P("gx", "gy", None, None),
        P("gx", "gy", None, None, None, None),
        P("gx", "gy", None, None),
        P(),
    )
    out_specs = (P("gx", "gy", None, None, None), P())
    return jax.shard_map(shards, mesh=mesh, in_specs=in_specs, out_specs=out_specs, check_vma=False)
```

```python
import functools

import jax
import jax.numpy as jnp
from jax import lax
from jax.experimental import pallas as pl
from jax.experimental.pallas import tpu as pltpu
from jax.sharding import PartitionSpec as P

MESH = pl.DeviceIdType.MESH
f32, bf16 = jnp.float32, jnp.bfloat16
NN = (((1,), (0,)), ((), ()))
NT = (((1,), (1,)), ((), ()))
ROWS, NB, COLS, TILE, FROWS = 64, 4, 16, 128, 24
GROUP = 8
NGROUPS = ROWS // GROUP
LOCAL = ROWS * NB
SLOTS = 4
BIG = 16
TERMS = 336


def dot(a, b, dims=NN):
    return lax.dot_general(a, b, dims, preferred_element_type=f32)


def split(x):
    high = x.astype(bf16)
    return high, (x - high.astype(f32)).astype(bf16)


def stacked(x):
    return jnp.concatenate(split(x), axis=0)


def times(pair, high, low, dims=NN):
    both = dot(pair, high, dims)
    return both[:COLS] + both[COLS:] + dot(pair[:COLS], low, dims)


def times_wide(pair, both):
    out = dot(pair, both)
    out = out[:COLS] + out[COLS:]
    return out[:, :TILE] + out[:, TILE:]


def exact(a, b, dims):
    return lax.dot_general(
        a, b, dims, precision=lax.Precision.HIGHEST, preferred_element_type=f32
    )


def kernel(
    gx, gy,
    cols_h, rows_h, bounds_h, diag_h, start_h, tiles_h, faces_h,
    basis_h, proj,
    cols_s, rows_s, bounds_s, cols_v, rows_v, diag, stage, fstage,
    tn_h0, tn_l0, tt_h0, tt_l0, tn_h1, tn_l1, tt_h1, tt_l1, cn, ct,
    vb, vs, acc, scat, terms, low, down_s, down_r, up_s, hot, places, ys, fys,
    pad, gbuf0, gbuf1, sbuf0, sbuf1,
    stage_sem, fstage_sem, start_sem, small_sem, out_sem,
    down_ss, down_rs, up_ss, up_rs, red_ss, red_rs,
):
    u, v = lax.axis_index("gx"), lax.axis_index("gy")
    held = (tn_h0, tn_l0, tt_h0, tt_l0), (tn_h1, tn_l1, tt_h1, tt_l1)
    nodes = float(gx * gy * ROWS * TILE)

    def stage_copy(group):
        slot = lax.rem(group, SLOTS)
        return pltpu.make_async_copy(
            tiles_h.at[pl.ds(group * GROUP, GROUP)], stage.at[slot], stage_sem.at[slot]
        )

    pairs = (
        (cols_h, cols_v), (rows_h, rows_v), (rows_h, rows_s), (cols_h, cols_s),
        (bounds_h, bounds_s), (diag_h, diag),
    )
    small = [pltpu.make_async_copy(a, b, small_sem.at[n]) for n, (a, b) in enumerate(pairs)]
    for copy in small[:2]:
        copy.start()
    start_copy = pltpu.make_async_copy(start_h, vb.at[0], start_sem)
    start_copy.start()
    for copy in small[2:]:
        copy.start()
    face_copies = [
        pltpu.make_async_copy(
            faces_h.at[pl.ds(axis * FROWS, FROWS)],
            fstage.at[pl.ds(axis * FROWS, FROWS)],
            fstage_sem.at[axis],
        )
        for axis in range(2)
    ]
    face_copies[1].start()
    face_copies[0].start()

    def past(me, step, size):
        other = me + step
        return jnp.where(other >= size, other - size, other)

    sums = (
        (gx, u, [(past(u, step, gx), v) for step in range(1, gx)]),
        (gy, v, [(u, past(v, step, gy)) for step in range(1, gy)]),
    )
    lower = sums[0][2][gx - 2], sums[1][2][gy - 2]
    upper = sums[0][2][0], sums[1][2][0]
    barrier = pltpu.get_barrier_semaphore()
    greeted = sums[0][2] + sums[1][2]
    for peer in greeted:
        pl.semaphore_signal(barrier, inc=1, device_id=peer, device_id_type=MESH)

    def down_copy(axis, slot):
        return pltpu.make_async_remote_copy(
            src_ref=down_s.at[slot, axis], dst_ref=down_r.at[slot, axis],
            send_sem=down_ss.at[slot, axis], recv_sem=down_rs.at[slot, axis],
            device_id=lower[axis], device_id_type=MESH,
        )

    def up_copy(axis, slot):
        return pltpu.make_async_remote_copy(
            src_ref=up_s.at[slot, axis], dst_ref=low.at[slot, axis],
            send_sem=up_ss.at[slot, axis], recv_sem=up_rs.at[slot, axis],
            device_id=upper[axis], device_id_type=MESH,
        )

    tall = lax.broadcasted_iota(jnp.int32, (ROWS, FROWS), 0)
    taller = lax.broadcasted_iota(jnp.int32, (ROWS, ROWS), 0)
    for copy in small:
        copy.wait()
    for k in range(NB):
        match = (cols_v[k : k + 1, :] == taller).astype(f32)
        hot[:, k * ROWS : (k + 1) * ROWS] = match
    hot[:, LOCAL:] = jnp.zeros((ROWS, 128), f32)
    has_upper = ((u < gx - 1).astype(f32), (v < gy - 1).astype(f32))
    has_lower = ((u > 0).astype(f32), (v > 0).astype(f32))
    for axis in range(2):
        gain = (rows_v[2 * axis : 2 * axis + 1, :] == tall).astype(f32) * has_upper[axis]
        hot[:, LOCAL + axis * FROWS : LOCAL + (axis + 1) * FROWS] = gain
        lost = (rows_v[2 * axis + 1 : 2 * axis + 2, :] == tall).astype(f32) * has_lower[axis]
        hot[:, TERMS + axis * FROWS : TERMS + (axis + 1) * FROWS] = lost
    places[...] = hot[...].astype(bf16)
    terms[(LOCAL + 2 * FROWS) * COLS :, :] = jnp.zeros(
        ((TERMS - LOCAL - 2 * FROWS) * COLS, TILE), f32
    )
    pad[...] = jnp.zeros((COLS, 128), f32)

    low_end = jnp.full((COLS, TILE), bounds_s[0], f32)
    high_end = jnp.full((COLS, TILE), bounds_s[1], f32)
    inverse_half = 2.0 / (high_end - low_end)
    centre = (high_end + low_end) * 0.5

    start_copy.wait()

    def split_rows(i, _):
        vs[i] = stacked(vb[0, i])
        return 0

    lax.fori_loop(0, ROWS, split_rows, 0, unroll=8)

    def fill_down(k, slot):
        def one(j, _):
            for axis in range(2):
                down_s[slot, axis, j] = vb[k, rows_s[2 * axis + 1, j]]
            return 0

        lax.fori_loop(0, FROWS, one, 0, unroll=8)

    def products(slot, axis, first):
        def one(j, _):
            f = axis * FROWS + j
            if first:
                high, small = split(fstage[f])
                both = jnp.concatenate([high, small], axis=1)
                cn[f] = both
                ct[f, :, :TILE] = jnp.transpose(high)
                ct[f, :, TILE:] = jnp.transpose(small)
            else:
                both = cn[f]
            up_s[slot, axis, j] = times_wide(vs[rows_s[2 * axis, j]], both)
            return 0

        lax.fori_loop(0, FROWS, one, 0, unroll=True)

    def gather4(i):
        return jnp.concatenate([vs[cols_s[k, i]] for k in range(NB)], axis=1)

    def convert_row(part, t, slot, r):
        tn_h, tn_l, tt_h, tt_l = held[part]
        for k in range(NB):
            high, small = split(stage[slot, r, k])
            lanes = slice(k * TILE, (k + 1) * TILE)
            tn_h[t, :, lanes] = high
            tn_l[t, :, lanes] = small
            tt_h[t, lanes, :] = jnp.transpose(high)
            tt_l[t, lanes, :] = jnp.transpose(small)

    def full_row(part, t, i):
        tn_h, tn_l, tt_h, tt_l = held[part]
        acc[i] = times(gather4(i), tt_h[t], tt_l[t])
        back = times(vs[i], tn_h[t], tn_l[t])
        for k in range(NB):
            at = pl.multiple_of((k * ROWS + i) * COLS, COLS)
            terms[pl.ds(at, COLS), :] = back[:, k * TILE : (k + 1) * TILE]

    def gains(slot):
        def one(j, _):
            for axis in range(2):
                f = axis * FROWS + j
                at = pl.multiple_of((LOCAL + f) * COLS, COLS)
                terms[pl.ds(at, COLS), :] = times_wide(
                    stacked(down_r[slot, axis, j]), ct[f]
                )
            return 0

        lax.fori_loop(0, FROWS, one, 0, unroll=True)

    def scatter(slot):
        got = low.at[slot].reshape(2 * FROWS * COLS, TILE)
        for c in range(COLS):
            column = jnp.concatenate(
                [
                    terms[pl.ds(c, TERMS, stride=COLS), :],
                    got[pl.ds(c, 2 * FROWS, stride=COLS), :],
                ],
                axis=0,
            )
            out = dot(places[...], jnp.concatenate(split(column), axis=1))
            scat[pl.ds(c, ROWS, stride=COLS), :] = out[:, :TILE] + out[:, TILE:]

    def update(k, before, scale, keep):
        def one(i, _):
            block = vb[k, i]
            at = pl.multiple_of(i * COLS, COLS)
            applied = diag[pl.ds(i, 1), :] * block + acc[i] + scat[pl.ds(at, COLS), :]
            new = scale * (applied - centre * block)
            if keep:
                new = new - vb[before, i]
            vb[k + 1, i] = new
            vs[i] = stacked(new)
            return 0

        lax.fori_loop(0, ROWS, one, 0, unroll=BIG)

    def apply(k, first):
        slot = lax.rem(k, 2)
        fill_down(k, slot)
        if first:
            pl.semaphore_wait(barrier, len(greeted))
        down_copy(1, slot).start()
        down_copy(0, slot).start()
        for axis in (1, 0):
            if first:
                face_copies[axis].wait()
                if axis == 1:
                    for group in range(SLOTS):
                        stage_copy(group).start()
            products(slot, axis, first)
            up_copy(axis, slot).start()

        def convert_group(part, pair, r):
            convert_row(part, pair * GROUP + r, lax.rem(2 * pair + part, SLOTS), r)

        def full_group(part, pair, r):
            full_row(part, pair * GROUP + r, (2 * pair + part) * GROUP + r)

        if first:
            stage_copy(0).wait()
            for r in range(GROUP):
                convert_group(0, 0, r)

            def two_groups(pair, _):
                @pl.when(pair < NGROUPS // 2 - 2)
                def _():
                    stage_copy(2 * pair + 4).start()

                stage_copy(2 * pair + 1).wait()
                for r in range(GROUP):
                    convert_group(1, pair, r)
                    full_group(0, pair, r)

                @pl.when(pair < NGROUPS // 2 - 2)
                def _():
                    stage_copy(2 * pair + 5).start()

                stage_copy(2 * pair + 2).wait()
                for r in range(GROUP):
                    convert_group(0, pair + 1, r)
                    full_group(1, pair, r)
                return 0

            lax.fori_loop(0, NGROUPS // 2 - 1, two_groups, 0)
            last = NGROUPS // 2 - 1
            stage_copy(NGROUPS - 1).wait()
            for r in range(GROUP):
                convert_group(1, last, r)
                full_group(0, last, r)
            for r in range(GROUP):
                full_group(1, last, r)
        else:

            def plain(two, _):
                for pair in (2 * two, 2 * two + 1):
                    for part in range(2):
                        for r in range(GROUP):
                            full_group(part, pair, r)
                return 0

            lax.fori_loop(0, NGROUPS // 4, plain, 0)
        for axis in range(2):
            down_copy(axis, slot).wait()
        gains(slot)
        for axis in range(2):
            up_copy(axis, slot).wait()
        scatter(slot)

    apply(0, True)
    update(0, 0, inverse_half, False)

    def later(k, _):
        apply(k, False)
        update(k, k - 1, 2.0 * inverse_half, True)
        return 0

    lax.fori_loop(1, 3, later, 0)

    def pack(x):
        pad[:, 0 : 2 * COLS] = x[:COLS] + x[COLS:]
        full = pad[...]
        full = jnp.where(at < COLS, full + pltpu.roll(full, 128 - COLS, 1), 0.0)
        return full[:8] + pltpu.roll(full[8:], 64, 1)

    lanes = lax.broadcasted_iota(jnp.int32, (8, 128), 1)
    at = lax.broadcasted_iota(jnp.int32, (COLS, 128), 1)

    def unpack(p):
        top = jnp.where(lanes < COLS, p, 0.0)
        bottom = jnp.where(lanes < COLS, pltpu.roll(p, 64, 1), 0.0)
        return jnp.concatenate([top, bottom], axis=0)

    buffers = (gbuf0, gbuf1), (sbuf0, sbuf1)

    def reduce_copies(which, stage_no):
        _, me, peers = sums[stage_no]
        own = buffers[which][stage_no].at[me]
        base = (which * 2 + stage_no) * gy
        return [
            pltpu.make_async_remote_copy(
                src_ref=own, dst_ref=own,
                send_sem=red_ss.at[base + n], recv_sem=red_rs.at[base + n],
                device_id=peer, device_id_type=MESH,
            )
            for n, peer in enumerate(peers)
        ]

    def reduce_start(which, stage_no, value):
        buffers[which][stage_no][sums[stage_no][1]] = value
        copies = reduce_copies(which, stage_no)
        far = [(abs((n + 1) % 4 - 2) + abs((n + 1) // 4 - 2), n) for n in range(len(copies))]
        for _, n in sorted(far):
            copies[n].start()

    def reduce_end(which, stage_no):
        size = sums[stage_no][0]
        copies = reduce_copies(which, stage_no)
        for copy in copies:
            copy.wait_send()
        for copy in copies:
            copy.wait_recv()
        parts = [buffers[which][stage_no][source] for source in range(size)]
        while len(parts) > 1:
            parts = [a + b for a, b in zip(parts[0::2], parts[1::2])]
        return parts[0]

    def inner(count, left, right):
        total = jnp.zeros((2 * COLS, 2 * COLS), f32)
        for g in range(count // BIG):
            a = jnp.concatenate([left(g * BIG + r) for r in range(BIG)], axis=1)
            b = jnp.concatenate([right(g * BIG + r) for r in range(BIG)], axis=1)
            total = total + dot(a, b, NT)
        return total

    fill_down(3, 1)
    down_copy(1, 1).start()
    down_copy(0, 1).start()
    gram = inner(ROWS, lambda i: vs[i], lambda i: vs[i])
    reduce_start(0, 0, pack(gram))

    def half_groups(pair, _):
        for part in range(2):
            high, small = held[part][2:]
            for r in range(GROUP):
                i = (2 * pair + part) * GROUP + r
                t = pair * GROUP + r
                image = times(gather4(i), high[t], small[t])
                image = image + 0.5 * (diag[pl.ds(i, 1), :] * vb[3, i])
                ys[i] = stacked(image)
        return 0

    lax.fori_loop(0, NGROUPS // 4, lambda two, c: half_groups(2 * two + 1, half_groups(2 * two, c)), 0)
    reduce_start(0, 1, reduce_end(0, 0))
    half = inner(ROWS, lambda i: vs[i], lambda i: ys[i])
    for axis in range(2):
        down_copy(axis, 1).wait()

    def half_face(j, _):
        for axis in range(2):
            f = axis * FROWS + j
            image = times_wide(stacked(down_r[1, axis, j]), ct[f])
            fys[f] = stacked(image * has_upper[axis])
        return 0

    lax.fori_loop(0, FROWS, half_face, 0, unroll=True)
    half = half + inner(
        2 * FROWS, lambda f: vs[rows_s[2 * (f // FROWS), f % FROWS]], lambda f: fys[f]
    )
    reduce_start(1, 0, pack(half))
    reduce_start(1, 1, reduce_end(1, 0))

    work = unpack(reduce_end(0, 1)) * (1.0 / nodes)
    down = lax.broadcasted_iota(jnp.int32, (COLS, 128), 0)
    work = work + (at == down + 64).astype(f32)
    for j in range(COLS):
        pivot = work[j : j + 1, :]
        root = 1.0 / jnp.sqrt(pivot[:, j : j + 1])
        pivot = pivot * root
        factor = work[:, j : j + 1] * root
        work = jnp.where(down > j, work - factor * pivot, jnp.where(down == j, pivot, work))
    inverse = jnp.where(at < COLS, pltpu.roll(work, 64, 1), 0.0)
    high, small = split(inverse)
    twice = high.astype(f32)
    twice = twice + pltpu.roll(twice, COLS, 1)
    mixer = jnp.concatenate([twice.astype(bf16), small], axis=0)[:, : 2 * COLS]


    for g in range(ROWS // 4):
        four = jnp.concatenate([vs[g * 4 + r] for r in range(4)], axis=1)
        out = dot(mixer, four)
        out = out[:COLS] + out[COLS:]
        for r in range(4):
            vb[0, g * 4 + r] = out[:, r * TILE : (r + 1) * TILE]
    out_copy = pltpu.make_async_copy(vb.at[0], basis_h, out_sem)
    out_copy.start()

    summed = unpack(reduce_end(1, 1))[:, :COLS] * (1.0 / nodes)
    narrow = inverse[:, :COLS]
    both = exact(narrow, summed, NN) + exact(narrow, summed, NT)
    proj[...] = exact(both, narrow, NT)
    out_copy.wait()


def hand_over(basis_in, proj_in, basis, proj, held, small, sems):
    parts = ROWS // BIG
    ins = [
        pltpu.make_async_copy(
            basis_in.at[pl.ds(g * BIG, BIG)], held.at[pl.ds(g * BIG, BIG)], sems.at[0, g]
        )
        for g in range(parts)
    ] + [pltpu.make_async_copy(proj_in, small, sems.at[0, parts])]
    outs = [
        pltpu.make_async_copy(
            held.at[pl.ds(g * BIG, BIG)], basis.at[pl.ds(g * BIG, BIG)], sems.at[1, g]
        )
        for g in range(parts)
    ] + [pltpu.make_async_copy(small, proj, sems.at[1, parts])]
    for copy in ins:
        copy.start()
    for first, second in zip(ins, outs):
        first.wait()
        second.start()
    for copy in outs:
        copy.wait()


def run(gx, gy, cols, rows, bounds, diag, start, tiles, faces):
    hbm = pl.BlockSpec(memory_space=pl.ANY)
    vmem = pl.BlockSpec(memory_space=pltpu.VMEM)
    faces_n = 2 * FROWS
    shapes = (
        jax.ShapeDtypeStruct((ROWS, COLS, TILE), f32),
        jax.ShapeDtypeStruct((COLS, COLS), f32),
    )
    results = pl.pallas_call(
        functools.partial(kernel, gx, gy),
        out_shape=shapes,
        in_specs=[hbm] * 7,
        out_specs=(hbm, vmem),
        scratch_shapes=[
            pltpu.SMEM((NB, ROWS), jnp.int32),
            pltpu.SMEM((4, FROWS), jnp.int32),
            pltpu.SMEM((2,), f32),
            pltpu.VMEM((NB, ROWS), jnp.int32),
            pltpu.VMEM((4, FROWS), jnp.int32),
            pltpu.VMEM((ROWS, TILE), f32),
            pltpu.VMEM((SLOTS, GROUP, NB, TILE, TILE), f32),
            pltpu.VMEM((faces_n, TILE, TILE), f32),
            *(
                [pltpu.VMEM((ROWS // 2, TILE, NB * TILE), bf16)] * 2
                + [pltpu.VMEM((ROWS // 2, NB * TILE, TILE), bf16)] * 2
            )
            * 2,
            pltpu.VMEM((faces_n, TILE, 2 * TILE), bf16),
            pltpu.VMEM((faces_n, TILE, 2 * TILE), bf16),
            pltpu.VMEM((4, ROWS, COLS, TILE), f32),
            pltpu.VMEM((ROWS, 2 * COLS, TILE), bf16),
            pltpu.VMEM((ROWS, COLS, TILE), f32),
            pltpu.VMEM((ROWS * COLS, TILE), f32),
            pltpu.VMEM((TERMS * COLS, TILE), f32),
            pltpu.VMEM((2, 2, FROWS, COLS, TILE), f32),
            pltpu.VMEM((2, 2, FROWS, COLS, TILE), f32),
            pltpu.VMEM((2, 2, FROWS, COLS, TILE), f32),
            pltpu.VMEM((2, 2, FROWS, COLS, TILE), f32),
            pltpu.VMEM((ROWS, 384), f32),
            pltpu.VMEM((ROWS, 384), bf16),
            pltpu.VMEM((ROWS, 2 * COLS, TILE), bf16),
            pltpu.VMEM((faces_n, 2 * COLS, TILE), bf16),
            pltpu.VMEM((COLS, 128), f32),
            *(
                pltpu.VMEM((gx, 8, 128), f32),
                pltpu.VMEM((gy, 8, 128), f32),
            )
            * 2,
            pltpu.SemaphoreType.DMA((SLOTS,)),
            pltpu.SemaphoreType.DMA((2,)),
            pltpu.SemaphoreType.DMA,
            pltpu.SemaphoreType.DMA((6,)),
            pltpu.SemaphoreType.DMA,
            pltpu.SemaphoreType.DMA((2, 2)),
            pltpu.SemaphoreType.DMA((2, 2)),
            pltpu.SemaphoreType.DMA((2, 2)),
            pltpu.SemaphoreType.DMA((2, 2)),
            pltpu.SemaphoreType.DMA((4 * gy,)),
            pltpu.SemaphoreType.DMA((4 * gy,)),
        ],
        compiler_params=pltpu.CompilerParams(
            collective_id=0, has_side_effects=True, vmem_limit_bytes=62 << 20
        ),
    )(cols, rows, bounds, diag, start, tiles, faces)
    return pl.pallas_call(
        hand_over,
        out_shape=shapes,
        in_specs=[hbm] * 2,
        out_specs=(hbm, hbm),
        scratch_shapes=[
            pltpu.VMEM((ROWS, COLS, TILE), f32),
            pltpu.VMEM((COLS, COLS), f32),
            pltpu.SemaphoreType.DMA((2, ROWS // BIG + 1)),
        ],
    )(*results)


def shards(start_block, tiles, tile_cols, node_diag, face_tiles, face_rows, filter_bounds):
    gx, gy = lax.axis_size("gx"), lax.axis_size("gy")
    basis, projected = run(
        gx, gy,
        tile_cols[0, 0].T, face_rows[0, 0], filter_bounds, node_diag[0, 0], start_block[0, 0],
        tiles[0, 0], face_tiles[0, 0].reshape(2 * FROWS, TILE, TILE),
    )
    return basis[None, None], projected


def solution(mesh):
    in_specs = (
        P("gx", "gy", None, None, None),
        P("gx", "gy", None, None, None, None),
        P("gx", "gy", None, None),
        P("gx", "gy", None, None),
        P("gx", "gy", None, None, None, None),
        P("gx", "gy", None, None),
        P(),
    )
    out_specs = (P("gx", "gy", None, None, None), P())
    return jax.shard_map(shards, mesh=mesh, in_specs=in_specs, out_specs=out_specs, check_vma=False)
```
